256 devices in a mesh: row: 32 (over z, x), col: 8 (over y, core).
Axes of the slice: x: 4, y: 4, z: 8, core: 2. Of those that a mesh axis runs over, the one named last changes fastest.
Arguments:
- trailing: float32 [2, 8192, 8, 2048], P(None, 'row', None, 'col'), may hold values from -6 to 6, as said below
- inv_block: float32 [256, 256], replicated, may hold values from -0.0625 to 0.4, as said below
- features: bfloat16 [8, 8, 256, 256], P(None, 'col'), may hold values from -6 to 6
- targets: float32 [2, 8192], P(None, 'row'), may hold values from -6 to 6
- cot_trailing: bfloat16 [2, 8192, 8, 2048], P(None, 'row', None, 'col'), may hold values from -6 to 6
Outputs:
- updated: float32 [2, 8192, 8, 2048], P(None, 'row', None, 'col')
- reduced_targets: float32 [2, 8192], P(None, 'row')
- grad_rows: float32 [2, 32, 256, 256], P(None, 'row', 'col')
- grad_cols: float32 [8, 8, 256, 256], P(None, 'col', 'row')
The draws below stay inside these ranges and needn't reach their ends.
Inputs may be any that keep to these rules, and one draw needn't show every extreme that they name: `inv_block`: lower triangular. `trailing`: symmetric when its dimensions 0 and 1 and its dimensions 2 and 3 are merged.
All inputs are finite; a program needn't handle non-finite values.
Results may differ from the reference program's by a relative error of at most 0.0024.
Values may be sent and summed in bfloat16 or wider, within the bound.
A program may use at most 128 MiB of HBM per device.

```python
import jax
import jax.numpy as jnp
from jax import lax

B = 256
F = 256
BR = 2
M = 16384
BC = 8
N_ROW = 32
N_COL = 8


def draw_trailing(key, part):
    order = BR * N_ROW * B
    noise = jax.random.normal(key, (order, order), jnp.float32)
    merged = jnp.clip((noise + noise.T) * 0.7071067811865476, -6.0, 6.0)
    return merged.reshape(BR, N_ROW * B, BC, N_COL * B).astype(jnp.float32)


def draw_inv_block(key, part):
    diag_key, fill_key = jax.random.split(key)
    row_ids = jnp.arange(B)[:, None]
    col_ids = jnp.arange(B)[None, :]
    diagonal = jnp.exp(jax.random.uniform(diag_key, (B,), jnp.float32, jnp.log(0.1), jnp.log(0.4)))
    filler = jnp.clip(jax.random.normal(fill_key, (B, B), jnp.float32), -4.0, 4.0)
    filler = jnp.clip(filler * (0.25 / jnp.sqrt(jnp.float32(B))), -0.0625, 0.0625)
    lower = jnp.where(row_ids > col_ids, filler, 0.0)
    return (lower + jnp.where(row_ids == col_ids, diagonal[:, None], 0.0)).astype(jnp.float32)


def block_levels(key, shape, cuts, low, high):
    loudness, own = 1.0, jax.random.fold_in(key, 6)
    for position, shards_of in cuts:
        draws = jnp.exp(jax.random.uniform(jax.random.fold_in(own, position), (shards_of,), jnp.float32, low / len(cuts), high / len(cuts)))
        loudness = loudness * jnp.repeat(draws, shape[position] // shards_of).reshape([-1 if axis == position else 1 for axis in range(len(shape))])
    return loudness


def bell_draw(stream_key, dims, scale, most, pieces=(), held_as=jnp.bfloat16):
    values = jax.random.normal(stream_key, dims, jnp.float32) * scale
    if len(pieces) > 0:
        values = block_levels(stream_key, dims, pieces, -0.22, 0.18) * values
    return jnp.clip(values, min=-most, max=most).astype(held_as)


def setup_inputs(seed: int = 0) -> dict:
    splits = jax.random.split(jax.random.key(seed), 6)
    trailing = draw_trailing(jax.random.fold_in(splits[5], 71), 0)
    inv_block = draw_inv_block(jax.random.fold_in(splits[5], 71), 0)
    features = bell_draw(splits[2], (BC, N_COL, B, F), 1.0, 6.0, ((1, 8),))
    targets = bell_draw(splits[3], (BR, N_ROW * B), 1.0, 6.0, ((1, 32),), jnp.float32)
    cot_trailing = bell_draw(splits[4], (BR, N_ROW * B, BC, N_COL * B), 1.0, 6.0, ((1, 32), (3, 8)))
    return dict(trailing=trailing, inv_block=inv_block, features=features, targets=targets, cot_trailing=cot_trailing)


def reference(trailing, inv_block, features, targets, cot_trailing):
    highest = lax.Precision.HIGHEST
    matrix = trailing.reshape(M, M)
    cotangent = cot_trailing.reshape(M, M)
    feature_mat = features.reshape(M, F)
    target_vec = targets.reshape(M)
    retained = (jnp.arange(M) >= B).astype(jnp.float32)
    lower_panel = jnp.dot(matrix[:, :B], inv_block.T, precision=highest) * retained[:, None]
    upper_panel = jnp.dot(inv_block, matrix[:B, :], precision=highest) * retained[None, :]
    updated = matrix - jnp.dot(lower_panel, upper_panel, precision=highest)
    solved = jnp.dot(inv_block, target_vec[:B], precision=highest)
    reduced = target_vec - jnp.dot(lower_panel, solved, precision=highest)
    lower_short = lower_panel.astype(jnp.bfloat16)
    upper_short = upper_panel.astype(jnp.bfloat16)
    lower_grad = -jnp.dot(cotangent, upper_short.T, preferred_element_type=jnp.float32)
    upper_grad = -jnp.dot(lower_short.T, cotangent, preferred_element_type=jnp.float32)
    column_adj = jnp.dot(lower_grad, inv_block, precision=highest) * retained[:, None]
    row_adj = jnp.dot(inv_block.T, upper_grad, precision=highest) * retained[None, :]
    feat_float = feature_mat.astype(jnp.float32)
    first_feats = feat_float[:B]
    rows_total = jnp.dot(cotangent, feature_mat, preferred_element_type=jnp.float32)
    rows_total = rows_total + jnp.dot(column_adj, first_feats, precision=highest)
    rows_total = rows_total.at[:B].add(jnp.dot(row_adj, feat_float, precision=highest))
    cols_total = jnp.dot(cotangent.T, feature_mat, preferred_element_type=jnp.float32)
    cols_total = cols_total + jnp.dot(row_adj.T, first_feats, precision=highest)
    cols_total = cols_total.at[:B].add(jnp.dot(column_adj.T, feat_float, precision=highest))
    grad_rows = (rows_total / F).reshape(BR, N_ROW, B, F)
    grad_cols = (cols_total / F).reshape(BC, N_COL, B, F)
    return updated.reshape(trailing.shape), reduced.reshape(targets.shape), grad_rows, grad_cols
```

```python
import functools

import jax
import jax.numpy as jnp
from jax import lax
from jax.experimental import pallas as pl
from jax.experimental.pallas import tpu as pltpu
from jax.sharding import PartitionSpec as P

MESH = pl.DeviceIdType.MESH
F32 = jnp.float32
BF16 = jnp.bfloat16
HIGHEST = lax.Precision.HIGHEST
NX, NZ, NY = 4, 8, 4


def mm(a, b):
    return jnp.dot(a, b, preferred_element_type=F32)


def mm_full(a, b):
    return jnp.dot(a, b, precision=HIGHEST, preferred_element_type=F32)


def split(v):
    hi = v.astype(BF16)
    return hi, (v - hi.astype(F32)).astype(BF16)


class Sends:
    def __init__(self, sems):
        self.sems = sems
        self.used = 0
        self.copies = []

    def make(self, src, dst, recv, device, slot=None):
        if slot is None:
            slot = self.used
            self.used += 1
        return pltpu.make_async_remote_copy(
            src_ref=src, dst_ref=dst, send_sem=self.sems.at[slot], recv_sem=recv,
            device_id=device, device_id_type=MESH,
        )

    def send(self, pred, src, dst, recv, device):
        copy = self.make(src, dst, recv, device)
        self.copies.append((pred, copy))
        if pred is None:
            copy.start()
        else:
            pl.when(pred)(copy.start)

    def drain(self):
        for pred, copy in self.copies:
            if pred is None:
                copy.wait_send()
            else:
                pl.when(pred)(copy.wait_send)


def arrived(ref, sem):
    pltpu.make_async_copy(ref, ref, sem).wait()


def comm_kernel(
    tr, inv, feats, y0, g,
    ls_out, llo_out, ut_out, rows_out, cols_out, red_out,
    g16, g32, gm, gt, xc, ls, llo, xr, x0, ut, y0b,
    wr, wc, mh, lst,
    part, pm1, pright, pleft, rm1, rleft, rright, zs, zr,
    rb, rsib, rys, ryr, es, esr, eu, eur, el, elr, euf, eufr, elf, elfr,
    acc,
    local_sem, send_sem, s1_sem, ua_sem, uz_sem, ux_sem,
    cs_sem, m1_sem, m2l_sem, m2r_sem, zss_sem, zr_sem,
    sib_sem, ry_sem, es_sem, eu_sem, el_sem, euf_sem, elf_sem, y0_sem,
):
    r = lax.axis_index("row")
    c = lax.axis_index("col")
    z, x = r // NX, r % NX
    y, k = c // 2, c % 2
    xr_, xl_, xo_ = (x + 1) % NX, (x + 3) % NX, (x + 2) % NX

    def at(z_, x_, c_):
        return (z_ * NX + x_, c_)

    sib = at(z, x, 2 * y + 1 - k)
    S = Sends(send_sem)

    get_g = pltpu.make_async_copy(g, g16, local_sem.at[0])
    get_f = pltpu.make_async_copy(feats, xc, local_sem.at[1])
    get_t = [pltpu.make_async_copy(tr.at[:, pl.ds(h * 128, 128)], g32.at[h], local_sem.at[2 + 4 * h]) for h in range(2)]

    @pl.when(c == 0)
    def _():
        get_t[0].start()
        get_t[1].start()

    get_f.start()
    get_g.start()

    def by_stride(b):
        s = pl.ds(b, 512, stride=8)
        return jnp.concatenate([g32.at[0][s, :], g32.at[1][s, :]], axis=1)

    bar = pltpu.get_barrier_semaphore()
    pl.semaphore_signal(bar, inc=1, device_id=sib, device_id_type=MESH)
    for d in range(1, NY):
        pl.semaphore_signal(bar, inc=1, device_id=at(z, x, 2 * ((y + d) % NY) + k), device_id_type=MESH)
    for d in range(1, NX):
        pl.semaphore_signal(bar, inc=1, device_id=at(z, (x + d) % NX, c), device_id_type=MESH)
    for d in range(1, NZ):
        pl.semaphore_signal(bar, inc=1, device_id=at((z + d) % NZ, x, c), device_id_type=MESH)
    far = (z % 2 == 1) & (z >= 3)

    @pl.when((c == 0) & far)
    def _():
        pl.semaphore_signal(bar, inc=1, device_id=at(z, x, z), device_id_type=MESH)

    pl.semaphore_wait(bar, 14 + jnp.where((c == z) & far, 1, 0))

    keep_row = jnp.where(r == 0, 0.0, 1.0).astype(F32)
    keep_col = jnp.where(c == 0, 0.0, 1.0).astype(F32)

    def piece(ref, q):
        n = ref.shape[0] // NY
        return ref.at[pl.ds(pl.multiple_of(q * n, n), n)]

    def bcast_root(ref, which, yr, kr):
        root = (y == yr) & (k == kr)
        sems = s1_sem.at[which]
        for d in range(1, NY):
            q = (yr + d) % NY
            S.send(root, piece(ref, q), piece(ref, q), sems.at[d], at(z, x, 2 * q + kr))
        for d in range(1, NY):
            q = (yr + d) % NY
            S.send(root, piece(ref, yr), piece(ref, yr), sems.at[0], at(z, x, 2 * q + kr))
        for d in range(NY):
            q = (yr + d) % NY
            S.send(root, piece(ref, q), piece(ref, q), sems.at[d], sib)

    def bcast_own(ref, which, yr, kr):
        relay = (y != yr) & (k == kr)
        sems = s1_sem.at[which]
        d0 = (y - yr + NY) % NY
        mine = piece(ref, y)
        pl.when(relay)(lambda: arrived(mine, sems.at[d0]))
        for e in (d0 % 3 + 1, (d0 + 1) % 3 + 1):
            S.send(relay, mine, mine, sems.at[d0], at(z, x, 2 * ((yr + e) % NY) + kr))
        S.send(relay, mine, mine, sems.at[d0], sib)

    def bcast_rest(ref, which, yr, kr):
        relay = (y != yr) & (k == kr)
        sems = s1_sem.at[which]
        d0 = (y - yr + NY) % NY
        for e in (d0 * 0, d0 % 3 + 1, (d0 + 1) % 3 + 1):
            p = piece(ref, (yr + e) % NY)
            pl.when(relay)(functools.partial(arrived, p, sems.at[e]))
            S.send(relay, p, p, sems.at[e], sib)

        @pl.when(k != kr)
        def _():
            for e in range(NY):
                arrived(piece(ref, (yr + e) % NY), sems.at[e])

    cr = r % 8
    yr2, kr2 = cr // 2, cr % 2
    b0 = r // 8

    get_f.wait()

    @pl.when(c == cr)
    def _():
        xr[pl.ds(0, 256), :] = xc[pl.ds(pl.multiple_of(b0 * 256, 256), 256), :]
        xr[pl.ds(256, 256), :] = xc[pl.ds(pl.multiple_of(b0 * 256 + 1024, 256), 256), :]

    bcast_root(xr, 2, yr2, kr2)

    @pl.when(c == 0)
    def _():
        x0[...] = xc[pl.ds(0, 256), :]

    bcast_root(x0, 1, 0, 0)

    @pl.when(c == 0)
    def _():
        get_t[0].wait()
        get_t[1].wait()
        a = by_stride(0)
        low = mm_full(a, inv[...].T)
        keep = jnp.where((r == 0) & (lax.broadcasted_iota(jnp.int32, (512, 256), 0) < 256), 0.0, 1.0)
        hi, lo = split(low * keep.astype(F32))
        ls[...] = hi
        llo[...] = lo

    bcast_root(ls, 0, 0, 0)

    first = (z == 0) & (x == 0)

    @pl.when(first)
    def _():
        y0b[...] = y0[...]

    for d in range(1, NZ):
        S.send(first, y0b, y0b, y0_sem.at[0], at((z + d) % NZ, x, c))

    get_g.wait()

    @pl.loop(0, 8)
    def _(i):
        s = pl.ds(pl.multiple_of(i * 512, 512), 512)
        v = g16[s, :].astype(F32)
        g32[0, s, :] = v[:, :128]
        g32[1, s, :] = v[:, 128:]

    def relayout(b):
        v = by_stride(b).astype(BF16)
        gm[:, b * 256:(b + 1) * 256] = v
        gt[b] = v.T

    relayout(0)
    bcast_own(xr, 2, yr2, kr2)
    bcast_own(x0, 1, 0, 0)
    relayout(1)
    relayout(2)
    relayout(3)
    bcast_own(ls, 0, 0, 0)
    bcast_rest(xr, 2, yr2, kr2)
    bcast_rest(x0, 1, 0, 0)
    relayout(4)
    relayout(5)
    bcast_rest(ls, 0, 0, 0)

    def slot(s, x_):
        return ut.at[s + 4 * (x_ // 2), x_ % 2]

    srow = (z % 2) == (c // 4)
    source = srow & (x == c % 4)
    mys = z // 2
    for d in range(1, NX):
        xd = (x + d) % NX
        S.send(source, ls.at[pl.ds(pl.multiple_of(xd * 128, 128), 128)], slot(mys, xd), ua_sem.at[0], at(z, xd, c))

    @pl.when(source)
    def _():
        ut[mys + 4 * (x // 2), x % 2] = ls[pl.ds(pl.multiple_of(x * 128, 128), 128), :]

    bcast_root(llo, 3, 0, 0)

    relayout(6)
    relayout(7)

    own = slot(mys, x)
    pl.when(srow & (x != c % 4))(lambda: arrived(own, ua_sem.at[0]))
    for d in range(1, NZ):
        S.send(srow, own, own, uz_sem.at[mys], at((z + d) % NZ, x, c))

    pl.when((x == 0) & (z != 0))(lambda: arrived(y0b, y0_sem.at[0]))
    for d in range(1, NX):
        S.send(x == 0, y0b, y0b, y0_sem.at[1], at(z, (x + d) % NX, c))

    mapped = mm_full(inv[...], x0[...].astype(F32))
    hi, lo = split(mapped)
    mh[0] = hi
    mh[1] = lo
    lst[...] = ls[...].T
    hi, lo = split(mm(ls[...], mh[0]) + mm(ls[...], mh[1]))
    wr[0] = hi
    wr[1] = lo

    def cols_block(b):
        keep = jnp.where((c == 0) & (b == 0), 0.0, 1.0).astype(F32)
        left = gt[b]
        v = mm(left, xr[...]) - keep * (mm(left, wr[0]) + mm(left, wr[1]))
        v = v.reshape(NZ, NX, 8, 256)
        for q in range(NX):
            part[q, b] = v[:, q].reshape(64, 256)

    def x_copy(src, dst, recv, which, i, device):
        return pltpu.make_async_remote_copy(
            src_ref=src, dst_ref=dst, send_sem=cs_sem.at[which, i], recv_sem=recv,
            device_id=device, device_id_type=MESH,
        )

    right, left_ = at(z, xr_, c), at(z, xl_, c)

    def step1(i):
        j = i + 4
        return (
            x_copy(pm1.at[i], rm1.at[i], m1_sem.at[i], 0, i, right),
            x_copy(pleft.at[i], rright.at[i], m2r_sem.at[i], 1, i, left_),
            x_copy(pm1.at[j], rm1.at[j], m1_sem.at[j], 2, i, left_),
            x_copy(pright.at[j], rleft.at[j], m2l_sem.at[j], 3, i, right),
        )

    def step2(i):
        j = i + 4
        return (
            x_copy(pright.at[i], rleft.at[i], m2l_sem.at[i], 4, i, right),
            x_copy(pleft.at[j], rright.at[j], m2r_sem.at[j], 5, i, left_),
        )

    @pl.loop(0, 4)
    def _(i):
        cols_block(i)
        cols_block(i + 4)
        j = i + 4
        pm1[i] = part[xo_, i].astype(BF16)
        pleft[i] = part[xl_, i].astype(BF16)
        pm1[j] = part[xo_, j].astype(BF16)
        pright[j] = part[xr_, j].astype(BF16)
        for copy in step1(i):
            copy.start()

    bcast_own(llo, 3, 0, 0)

    for s in range(4):
        p = slot(s, x)
        pl.when(jnp.logical_not(srow & (mys == s)))(functools.partial(arrived, p, uz_sem.at[s]))
        S.send(None, p, p, ux_sem.at[0, s], right)
        S.send(None, p, p, ux_sem.at[1, s], left_)

    @pl.loop(0, 4)
    def _(i):
        j = i + 4
        arrived(rm1.at[i], m1_sem.at[i])
        pright[i] = (part[xr_, i] + rm1[i].astype(F32)).astype(BF16)
        arrived(rm1.at[j], m1_sem.at[j])
        pleft[j] = (part[xl_, j] + rm1[j].astype(F32)).astype(BF16)
        for copy in step2(i):
            copy.start()

    for s in range(4):
        p = slot(s, xl_)
        arrived(p, ux_sem.at[0, s])
        if s < 2:
            S.send(None, p, p, ux_sem.at[2, s], right)
        p = slot(s, xr_)
        arrived(p, ux_sem.at[1, s])
        if s >= 2:
            S.send(None, p, p, ux_sem.at[2, s], left_)

    bcast_rest(llo, 3, 0, 0)

    for blk in range(2):
        rsl = pl.ds(blk * 256, 256)
        first_col = mm(gm[rsl, :256], xc[:256, :])
        rest = mm(gm[rsl, 256:], xc[256:, :])
        acc[rsl, :] = rest + first_col
        hi, lo = split(rest + keep_col * first_col)
        wc[0, rsl, :] = hi
        wc[1, rsl, :] = lo
    upper = mm(lst[...], wc[0, :512, :]) + mm(lst[...], wc[1, :512, :])
    invt = inv[...].T
    upper = -mm_full(invt, upper)
    for q in range(8):
        rb[q % 2, q // 2, 2] = upper[q * 32:(q + 1) * 32, :]

    def z_copy(i, d):
        zd = (z + d) % NZ
        return pltpu.make_async_remote_copy(
            src_ref=zs.at[zd, i], dst_ref=zr.at[z, i], send_sem=zss_sem.at[i, d], recv_sem=zr_sem.at[i, z],
            device_id=at(zd, x, c), device_id_type=MESH,
        )

    @pl.loop(0, 4)
    def _(i):
        for h in range(2):
            b = i + 4 * h
            arrived(rleft.at[b], m2l_sem.at[b])
            arrived(rright.at[b], m2r_sem.at[b])
            v = part[x, b] + rleft[b].astype(F32) + rright[b].astype(F32)
            v = v.reshape(NZ, 8, 256)
            for q in range(NZ):
                zs[q, i, h] = v[q]
        for d in range(1, NZ):
            z_copy(i, d).start()

    pl.when(x != 0)(lambda: arrived(y0b, y0_sem.at[1]))
    solved = mm_full(y0b[...], inv[...].T)
    lower_full = ls[...].astype(F32) + llo[...].astype(F32)
    red_out[...] = lax.dot_general(
        solved, lower_full, (((1,), (1,)), ((), ())), precision=HIGHEST, preferred_element_type=F32
    )

    for s in range(4):
        arrived(slot(s, xo_), ux_sem.at[2, s])
    put_u = pltpu.make_async_copy(ut, ut_out, local_sem.at[3])
    put_l = pltpu.make_async_copy(ls, ls_out, local_sem.at[4])
    put_o = pltpu.make_async_copy(llo, llo_out, local_sem.at[5])
    put_u.start()
    put_l.start()
    put_o.start()

    @pl.loop(0, 8)
    def _(b):
        s = pl.ds(pl.multiple_of(b * 256, 256), 256)
        u = ut[b].reshape(256, 256)
        hi, lo = split(mm(u, mh[0]) + mm(u, mh[1]))
        wc[0, s, :] = hi
        wc[1, s, :] = lo

    low_sum = jnp.zeros((256, 256), F32)
    whole = ut[...].reshape(2048, 256)
    for blk in range(2):
        rsl = pl.ds(blk * 256, 256)
        keep = keep_row if blk == 0 else jnp.ones((), F32)
        rows = acc[rsl, :] - keep * (mm(gm[rsl, :], wc[0]) + mm(gm[rsl, :], wc[1]))
        for q in range(8):
            rb[q % 2, q // 2, blk] = rows[q * 32:(q + 1) * 32, :]
        t = mm(gm[rsl, :], whole) * keep
        hi, lo = split(t.T)
        low_sum = low_sum + mm(hi, xr[rsl, :]) + mm(lo, xr[rsl, :])
    lower = -mm_full(invt, low_sum)
    for q in range(8):
        rb[q % 2, q // 2, 3] = lower[q * 32:(q + 1) * 32, :]

    S.send(None, rb.at[1 - k], rsib, sib_sem.at[0], sib)
    arrived(rsib, sib_sem.at[0])

    @pl.loop(0, 4)
    def _(q):
        v = rb[k, q] + rsib[q]
        rb[k, q] = v
        rys[q] = v.astype(BF16)

    for d in range(1, NY):
        q = (y + d) % NY
        S.send(None, rys.at[q], ryr.at[y], ry_sem.at[y], at(z, x, 2 * q + k))
    total = rb[k, y]
    for d in range(1, NY):
        q = (y + d) % NY
        arrived(ryr.at[q], ry_sem.at[q])
        total = total + ryr[q].astype(F32)
    rows_out[...] = total[:2]

    for q in range(NX):
        es[q] = total[2:, q * 8:(q + 1) * 8, :]
    for d in range(1, NX):
        q = (x + d) % NX
        S.send(None, es.at[q], esr.at[x], es_sem.at[x], at(z, q, c))
    pair = es[x]
    for d in range(1, NX):
        q = (x + d) % NX
        arrived(esr.at[q], es_sem.at[q])
        pair = pair + esr[q]
    eu[...] = pair[0]
    el[...] = pair[1]
    S.send(z != 0, eu, eur.at[z], eu_sem.at[z], at(0 * z, x, c))
    S.send(z != c, el, elr.at[z], el_sem.at[z], at(c, x, c))

    euf[...] = eu[...]

    @pl.when(z == 0)
    def _():
        v = eu[...]
        for q in range(1, NZ):
            arrived(eur.at[q], eu_sem.at[q])
            v = v + eur[q]
        euf[...] = v

    S.send((z == 0) & (x != 0), euf, eufr.at[x], euf_sem.at[x], at(z, 0 * x, c))

    elf[...] = el[...]

    @pl.when(z == c)
    def _():
        v = el[...]
        for d in range(1, NZ):
            q = (z + d) % NZ
            arrived(elr.at[q], el_sem.at[q])
            v = v + elr[q]
        elf[...] = v

    S.send((z == c) & (c != 0), elf, elfr, elf_sem.at[0], at(z, x, 0 * c))

    for i in range(4):
        v = zs[z, i]
        for d in range(1, NZ):
            q = (z + d) % NZ
            arrived(zr.at[q, i], zr_sem.at[i, q])
            v = v + zr[q, i]
        cols_out[i] = v[0]
        cols_out[i + 4] = v[1]

    @pl.when(c == 0)
    def _():
        @pl.when(z == 0)
        def _():
            cols_out[0] = cols_out[0] + elf[...]

        @pl.when(z != 0)
        def _():
            arrived(elfr, elf_sem.at[0])
            cols_out[0] = cols_out[0] + elfr[...]

    @pl.when((z == 0) & (x == 0))
    def _():
        rows_out[0, :8] = rows_out[0, :8] + euf[...]
        for q in range(1, NX):
            arrived(eufr.at[q], euf_sem.at[q])
            rows_out[0, q * 8:(q + 1) * 8] = rows_out[0, q * 8:(q + 1) * 8] + eufr[q]

    S.drain()

    @pl.loop(0, 4)
    def _(i):
        for copy in step1(i) + step2(i):
            copy.wait_send()
        for d in range(1, NZ):
            z_copy(i, d).wait_send()

    put_u.wait()
    put_l.wait()
    put_o.wait()


def update_kernel(a, lh, ll, u, out, mixed):
    for b in range(8):
        ub = u[b * 256:(b + 1) * 256, :]
        dims = (((1,), (1,)), ((), ()))
        v = lax.dot_general(lh[...], ub, dims, preferred_element_type=F32)
        v = v + lax.dot_general(ll[...], ub, dims, preferred_element_type=F32)
        s = pl.ds(b, lh.shape[0], stride=8)
        mixed.at[0][s, :] = v[:, :128]
        mixed.at[1][s, :] = v[:, 128:]
    out[:, :128] = a[:, :128] - mixed[0]
    out[:, 128:] = a[:, 128:] - mixed[1]


def shards(trailing, inv_block, features, targets, cot_trailing):
    tr = trailing.reshape(4096, 256)
    g = cot_trailing.reshape(4096, 256)
    feats = features.reshape(2048, 256)
    y0 = jnp.broadcast_to(targets[0][None, :], (8, 256))
    vm = pl.BlockSpec(memory_space=pltpu.VMEM)
    anyspace = pl.BlockSpec(memory_space=pl.ANY)
    V = pltpu.VMEM
    D = pltpu.SemaphoreType.DMA
    ls, llo, ut, rows, cols, red = pl.pallas_call(
        comm_kernel,
        out_shape=(
            jax.ShapeDtypeStruct((512, 256), BF16),
            jax.ShapeDtypeStruct((512, 256), BF16),
            jax.ShapeDtypeStruct((8, 2, 128, 256), BF16),
            jax.ShapeDtypeStruct((2, 32, 256), F32),
            jax.ShapeDtypeStruct((8, 8, 256), F32),
            jax.ShapeDtypeStruct((8, 512), F32),
        ),
        in_specs=[anyspace, vm, anyspace, vm, anyspace],
        out_specs=(anyspace, anyspace, anyspace, vm, vm, vm),
        scratch_shapes=[
            V((4096, 256), BF16), V((2, 4096, 128), F32), V((512, 2048), BF16), V((8, 256, 512), BF16),
            V((2048, 256), BF16), V((512, 256), BF16), V((512, 256), BF16), V((512, 256), BF16),
            V((256, 256), BF16), V((8, 2, 128, 256), BF16), V((8, 256), F32),
            V((2, 512, 256), BF16), V((2, 2048, 256), BF16), V((2, 256, 256), BF16), V((256, 512), BF16),
            V((4, 8, 64, 256), F32), V((8, 64, 256), BF16), V((8, 64, 256), BF16), V((8, 64, 256), BF16),
            V((8, 64, 256), BF16), V((8, 64, 256), BF16), V((8, 64, 256), BF16),
            V((8, 4, 2, 8, 256), F32), V((8, 4, 2, 8, 256), F32),
            V((2, 4, 4, 32, 256), F32), V((4, 4, 32, 256), F32), V((4, 4, 32, 256), BF16), V((4, 4, 32, 256), BF16),
            V((4, 2, 8, 256), F32), V((4, 2, 8, 256), F32),
            V((8, 256), F32), V((8, 8, 256), F32), V((8, 256), F32), V((8, 8, 256), F32),
            V((8, 256), F32), V((4, 8, 256), F32), V((8, 256), F32), V((8, 256), F32),
            V((512, 256), F32),
            D((7,)), D((128,)), D((4, 4)), D((1,)), D((4,)), D((3, 4)),
            D((6, 4)), D((8,)), D((8,)), D((8,)), D((4, 8)), D((4, 8)),
            D((1,)), D((4,)), D((4,)), D((8,)), D((8,)), D((4,)), D((1,)), D((2,)),
        ],
        compiler_params=pltpu.CompilerParams(
            collective_id=0, has_side_effects=True, vmem_limit_bytes=48 * 1024 * 1024
        ),
        name="panel_comm",
    )(tr, inv_block, feats, y0, g)
    tile = 64
    updated = pl.pallas_call(
        update_kernel,
        out_shape=jax.ShapeDtypeStruct((4096, 256), F32),
        grid=(512 // tile,),
        in_specs=[
            pl.BlockSpec((tile * 8, 256), lambda i: (i, 0)),
            pl.BlockSpec((tile, 256), lambda i: (i, 0)),
            pl.BlockSpec((tile, 256), lambda i: (i, 0)),
            pl.BlockSpec((2048, 256), lambda i: (0, 0)),
        ],
        out_specs=pl.BlockSpec((tile * 8, 256), lambda i: (i, 0)),
        scratch_shapes=[V((2, tile * 8, 128), F32)],
        compiler_params=pltpu.CompilerParams(vmem_limit_bytes=24 * 1024 * 1024),
        name="panel_update",
    )(tr, ls, llo, ut.reshape(2048, 256))
    reduced = targets - red[0].reshape(targets.shape)
    scale = 1.0 / features.shape[3]
    return (
        updated.reshape(trailing.shape),
        reduced,
        (rows * scale).reshape(2, 1, 32, 256),
        (cols * scale).reshape(8, 1, 8, 256),
    )


def solution(mesh):
    return jax.shard_map(
        shards,
        mesh=mesh,
        in_specs=(
            P(None, "row", None, "col"),
            P(),
            P(None, "col", None, None),
            P(None, "row"),
            P(None, "row", None, "col"),
        ),
        out_specs=(
            P(None, "row", None, "col"),
            P(None, "row"),
            P(None, "row", "col", None),
            P(None, "col", "row", None),
        ),
        check_vma=False,
    )
```

```python
import functools

import jax
import jax.numpy as jnp
from jax import lax
from jax.experimental import pallas as pl
from jax.experimental.pallas import tpu as pltpu
from jax.sharding import PartitionSpec as P

MESH = pl.DeviceIdType.MESH
F32 = jnp.float32
BF16 = jnp.bfloat16
HIGHEST = lax.Precision.HIGHEST
NX, NZ, NY = 4, 8, 4


def mm(a, b):
    return jnp.dot(a, b, preferred_element_type=F32)


def split(v):
    hi = v.astype(BF16)
    return hi, (v - hi.astype(F32)).astype(BF16)


def mm_full(a, b):
    ah, al = split(a)
    bh, bl = split(b)
    return mm(ah, bh) + (mm(ah, bl) + mm(al, bh))


class Sends:
    def __init__(self, sems):
        self.sems = sems
        self.used = 0
        self.copies = []

    def make(self, src, dst, recv, device, slot=None):
        if slot is None:
            slot = self.used
            self.used += 1
        return pltpu.make_async_remote_copy(
            src_ref=src, dst_ref=dst, send_sem=self.sems.at[slot], recv_sem=recv,
            device_id=device, device_id_type=MESH,
        )

    def send(self, pred, src, dst, recv, device):
        copy = self.make(src, dst, recv, device)
        self.copies.append((pred, copy))
        if pred is None:
            copy.start()
        else:
            pl.when(pred)(copy.start)

    def drain(self):
        for pred, copy in self.copies:
            if pred is None:
                copy.wait_send()
            else:
                pl.when(pred)(copy.wait_send)


def arrived(ref, sem):
    pltpu.make_async_copy(ref, ref, sem).wait()


def comm_kernel(
    tr, inv, feats, targets, g,
    up_out, red_out, rows_out, cols_out,
    g16, g32, gm, gt, xc, ls, llo, xr, x0, ut, y0b, up,
    wr, wc, mh, lst,
    part, pm1, pright, pleft, rm1, rleft, rright, zs, zr,
    rb, rsib, rys, ryr,
    ub, usib, uy, uyr, ux, uxr, uz, uzr, uf, ufr,
    lx, lxr, lz, lzr, lf, lfr,
    acc,
    local_sem, send_sem, s1_sem, ua_sem, uz_sem, ux_sem,
    cs_sem, m1_sem, m2l_sem, m2r_sem, zss_sem, zr_sem,
    sib_sem, ry_sem, up_sem, upy_sem, upx_sem, upz_sem, upf_sem, lowx_sem, lowz_sem, lowf_sem, y0_sem,
):
    r = lax.axis_index("row")
    c = lax.axis_index("col")
    z, x = r // NX, r % NX
    y, k = c // 2, c % 2
    xr_, xl_, xo_ = (x + 1) % NX, (x + 3) % NX, (x + 2) % NX

    def at(z_, x_, c_):
        return (z_ * NX + x_, c_)

    sib = at(z, x, 2 * y + 1 - k)
    S = Sends(send_sem)
    scale = 1.0 / feats.shape[1]

    get_g = pltpu.make_async_copy(g, g16, local_sem.at[0])
    get_f = pltpu.make_async_copy(feats, xc, local_sem.at[1])
    get_t = [pltpu.make_async_copy(tr.at[:, pl.ds(h * 128, 128)], g32.at[h], local_sem.at[2 + 6 * h]) for h in range(2)]

    @pl.when(c == 0)
    def _():
        get_t[0].start()
        get_t[1].start()

    get_f.start()
    get_a = pltpu.make_async_copy(tr, up, local_sem.at[3])

    @pl.when(c != 0)
    def _():
        get_g.start()
        get_a.start()

    def by_stride(b):
        s = pl.ds(b, 512, stride=8)
        return jnp.concatenate([g32.at[0][s, :], g32.at[1][s, :]], axis=1)

    bar = pltpu.get_barrier_semaphore()
    pl.semaphore_signal(bar, inc=1, device_id=sib, device_id_type=MESH)
    for d in range(1, NY):
        pl.semaphore_signal(bar, inc=1, device_id=at(z, x, 2 * ((y + d) % NY) + k), device_id_type=MESH)
    for d in range(1, NX):
        pl.semaphore_signal(bar, inc=1, device_id=at(z, (x + d) % NX, c), device_id_type=MESH)
    for d in range(1, NZ):
        pl.semaphore_signal(bar, inc=1, device_id=at((z + d) % NZ, x, c), device_id_type=MESH)
    srow = (z % 2) == (c // 4)
    home = c % 4
    cr = r % 8

    @pl.when(srow & jnp.logical_not((c == 0) & (x == home)))
    def _():
        pl.semaphore_signal(bar, inc=1, device_id=at(z, home, 0 * c), device_id_type=MESH)

    @pl.when(c == 0)
    def _():
        for q in (3, 5, 7):
            pl.semaphore_signal(bar, inc=1, device_id=at(z, x, q), device_id_type=MESH)

    pl.semaphore_wait(
        bar, 14 + jnp.where(c == 0, 4 - jnp.where(cr == 0, 1, 0), 0) + jnp.where((k == 1) & (c >= 3), 1, 0)
    )

    keep_row = jnp.where(r == 0, 0.0, 1.0).astype(F32)
    keep_col = jnp.where(c == 0, 0.0, 1.0).astype(F32)

    def piece(ref, q):
        n = ref.shape[0] // NY
        return ref.at[pl.ds(pl.multiple_of(q * n, n), n)]

    def bcast_root(ref, which, yr, kr):
        root = (y == yr) & (k == kr)
        sems = s1_sem.at[which]
        for d in range(1, NY):
            q = (yr + d) % NY
            S.send(root, piece(ref, q), piece(ref, q), sems.at[d], at(z, x, 2 * q + kr))
        for d in range(1, NY):
            q = (yr + d) % NY
            S.send(root, piece(ref, yr), piece(ref, yr), sems.at[0], at(z, x, 2 * q + kr))
        for d in range(NY):
            q = (yr + d) % NY
            S.send(root, piece(ref, q), piece(ref, q), sems.at[d], sib)

    def bcast_own(ref, which, yr, kr):
        relay = (y != yr) & (k == kr)
        sems = s1_sem.at[which]
        d0 = (y - yr + NY) % NY
        mine = piece(ref, y)
        pl.when(relay)(lambda: arrived(mine, sems.at[d0]))
        for e in (d0 % 3 + 1, (d0 + 1) % 3 + 1):
            S.send(relay, mine, mine, sems.at[d0], at(z, x, 2 * ((yr + e) % NY) + kr))
        S.send(relay, mine, mine, sems.at[d0], sib)

    def bcast_rest(ref, which, yr, kr):
        relay = (y != yr) & (k == kr)
        sems = s1_sem.at[which]
        d0 = (y - yr + NY) % NY
        for e in (d0 * 0, d0 % 3 + 1, (d0 + 1) % 3 + 1):
            p = piece(ref, (yr + e) % NY)
            pl.when(relay)(functools.partial(arrived, p, sems.at[e]))
            S.send(relay, p, p, sems.at[e], sib)

        @pl.when(k != kr)
        def _():
            for e in range(NY):
                arrived(piece(ref, (yr + e) % NY), sems.at[e])

    yr2, kr2 = cr // 2, cr % 2
    b0 = r // 8
    mys = z // 2

    def slot(s, x_):
        return ut.at[s + 4 * (x_ // 2), x_ % 2]

    @pl.when(c == 0)
    def _():
        get_t[0].wait()
        get_t[1].wait()
        low = mm_full(by_stride(0), inv[...].T)
        keep = jnp.where((r == 0) & (lax.broadcasted_iota(jnp.int32, (512, 256), 0) < 256), 0.0, 1.0)
        hi, lo = split(low * keep.astype(F32))
        ls[...] = hi
        llo[...] = lo

    for q in range(NX):
        mine = (cr == 0) & (x == q)
        chunk = ls.at[pl.ds(q * 128, 128)]
        S.send((c == 0) & jnp.logical_not(mine), chunk, slot(mys, q), ua_sem.at[0], at(z, q, cr))

        @pl.when((c == 0) & mine)
        def _():
            ut[mys + 4 * (q // 2), q % 2] = chunk[...]

    bcast_root(ls, 0, 0, 0)
    get_f.wait()

    @pl.when(c == 0)
    def _():
        get_g.start()
        get_a.start()
        x0[...] = xc[pl.ds(0, 256), :]

    bcast_root(x0, 1, 0, 0)

    @pl.when(c == cr)
    def _():
        xr[pl.ds(0, 256), :] = xc[pl.ds(pl.multiple_of(b0 * 256, 256), 256), :]
        xr[pl.ds(256, 256), :] = xc[pl.ds(pl.multiple_of(b0 * 256 + 1024, 256), 256), :]

    bcast_root(xr, 2, yr2, kr2)

    first = (z == 0) & (x == 0)

    @pl.when(first)
    def _():
        y0b[...] = jnp.broadcast_to(targets[0:1, :], (8, 256))

    for d in range(1, NZ):
        S.send(first, y0b, y0b, y0_sem.at[0], at((z + d) % NZ, x, c))

    def relayout(b):
        v = by_stride(b).astype(BF16)
        gm[:, b * 256:(b + 1) * 256] = v
        gt[b] = v.T

    get_g.wait()

    @pl.loop(0, 8)
    def _(i):
        s = pl.ds(pl.multiple_of(i * 512, 512), 512)
        v = g16[s, :].astype(F32)
        g32[0, s, :] = v[:, :128]
        g32[1, s, :] = v[:, 128:]

    own = slot(mys, x)
    pl.when(srow & jnp.logical_not((c == 0) & (x == home)))(lambda: arrived(own, ua_sem.at[0]))
    for d in range(1, NZ):
        S.send(srow, own, own, uz_sem.at[mys], at((z + d) % NZ, x, c))

    bcast_own(ls, 0, 0, 0)
    bcast_own(x0, 1, 0, 0)
    bcast_own(xr, 2, yr2, kr2)
    relayout(0)
    relayout(1)
    relayout(2)
    bcast_rest(ls, 0, 0, 0)
    bcast_rest(x0, 1, 0, 0)
    bcast_rest(xr, 2, yr2, kr2)
    for b in range(3, 8):
        relayout(b)

    right, left_ = at(z, xr_, c), at(z, xl_, c)

    for s in range(4):
        p = slot(s, x)
        pl.when(jnp.logical_not(srow & (mys == s)))(functools.partial(arrived, p, uz_sem.at[s]))
        S.send(None, p, p, ux_sem.at[0, s], right)
        S.send(None, p, p, ux_sem.at[1, s], left_)

    bcast_root(llo, 3, 0, 0)

    pl.when((x == 0) & (z != 0))(lambda: arrived(y0b, y0_sem.at[0]))
    for d in range(1, NX):
        S.send(x == 0, y0b, y0b, y0_sem.at[1], at(z, (x + d) % NX, c))

    mapped = mm_full(inv[...], x0[...].astype(F32))
    hi, lo = split(mapped)
    mh[0] = hi
    mh[1] = lo
    lst[...] = ls[...].T
    hi, lo = split(mm(ls[...], mh[0]) + mm(ls[...], mh[1]))
    wr[0] = hi
    wr[1] = lo

    def cols_block(b):
        keep = jnp.where((c == 0) & (b == 0), 0.0, 1.0).astype(F32)
        left = gt[b]
        v = mm(left, xr[...]) - keep * (mm(left, wr[0]) + mm(left, wr[1]))
        v = v.reshape(NZ, NX, 8, 256)
        for q in range(NX):
            part[q, b] = v[:, q].reshape(64, 256)

    def x_copy(src, dst, recv, which, i, device):
        return pltpu.make_async_remote_copy(
            src_ref=src, dst_ref=dst, send_sem=cs_sem.at[which, i], recv_sem=recv,
            device_id=device, device_id_type=MESH,
        )

    def step1(i):
        j = i + 4
        return (
            x_copy(pm1.at[i], rm1.at[i], m1_sem.at[i], 0, i, right),
            x_copy(pleft.at[i], rright.at[i], m2r_sem.at[i], 1, i, left_),
            x_copy(pm1.at[j], rm1.at[j], m1_sem.at[j], 2, i, left_),
            x_copy(pright.at[j], rleft.at[j], m2l_sem.at[j], 3, i, right),
        )

    def step2(i):
        j = i + 4
        return (
            x_copy(pright.at[i], rleft.at[i], m2l_sem.at[i], 4, i, right),
            x_copy(pleft.at[j], rright.at[j], m2r_sem.at[j], 5, i, left_),
        )

    def cols_step(i):
        cols_block(i)
        cols_block(i + 4)
        j = i + 4
        pm1[i] = part[xo_, i].astype(BF16)
        pleft[i] = part[xl_, i].astype(BF16)
        pm1[j] = part[xo_, j].astype(BF16)
        pright[j] = part[xr_, j].astype(BF16)
        for copy in step1(i):
            copy.start()

    def relay_upper(s):
        p = slot(s, xl_)
        arrived(p, ux_sem.at[0, s])
        if s < 2:
            S.send(None, p, p, ux_sem.at[2, s], right)
        p = slot(s, xr_)
        arrived(p, ux_sem.at[1, s])
        if s >= 2:
            S.send(None, p, p, ux_sem.at[2, s], left_)

    pl.loop(0, 2)(cols_step)
    for s in range(4):
        relay_upper(s)
    pl.loop(2, 4)(cols_step)

    @pl.loop(0, 4)
    def _(i):
        j = i + 4
        arrived(rm1.at[i], m1_sem.at[i])
        pright[i] = (part[xr_, i] + rm1[i].astype(F32)).astype(BF16)
        arrived(rm1.at[j], m1_sem.at[j])
        pleft[j] = (part[xl_, j] + rm1[j].astype(F32)).astype(BF16)
        for copy in step2(i):
            copy.start()

    bcast_own(llo, 3, 0, 0)
    bcast_rest(llo, 3, 0, 0)

    for blk in range(2):
        rsl = pl.ds(blk * 256, 256)
        first_col = mm(gm[rsl, :256], xc[:256, :])
        rest = mm(gm[rsl, 256:], xc[256:, :])
        acc[rsl, :] = rest + first_col
        hi, lo = split(rest + keep_col * first_col)
        wc[0, rsl, :] = hi
        wc[1, rsl, :] = lo
    upper = mm(lst[...], wc[0, :512, :]) + mm(lst[...], wc[1, :512, :])
    invt = inv[...].T
    upper = -mm_full(invt, upper)
    for q in range(8):
        ub[q % 2, q // 2] = upper[q * 32:(q + 1) * 32, :]
    S.send(None, ub.at[1 - k], usib, up_sem.at[0], sib)

    def z_copy(i, d):
        zd = (z + d) % NZ
        return pltpu.make_async_remote_copy(
            src_ref=zs.at[zd, i], dst_ref=zr.at[z, i], send_sem=zss_sem.at[i, d], recv_sem=zr_sem.at[i, z],
            device_id=at(zd, x, c), device_id_type=MESH,
        )

    @pl.loop(0, 4)
    def _(i):
        for h in range(2):
            b = i + 4 * h
            arrived(rleft.at[b], m2l_sem.at[b])
            arrived(rright.at[b], m2r_sem.at[b])
            v = part[x, b] + rleft[b].astype(F32) + rright[b].astype(F32)
            v = v.reshape(NZ, 8, 256)
            for q in range(NZ):
                zs[q, i, h] = v[q]
        for d in range(1, NZ):
            z_copy(i, d).start()

    def upper_y():
        arrived(usib, up_sem.at[0])
        uy[...] = ub[k] + usib[...]
        for d in range(1, NY):
            q = (y + d) % NY
            S.send(None, uy.at[q], uyr.at[y], upy_sem.at[y], at(z, x, 2 * q + k))

    def upper_x():
        v = uy[y]
        for d in range(1, NY):
            q = (y + d) % NY
            arrived(uyr.at[q], upy_sem.at[q])
            v = v + uyr[q]
        for q in range(NX):
            ux[q] = v[q * 8:(q + 1) * 8]
        for d in range(1, NX):
            q = (x + d) % NX
            S.send(None, ux.at[q], uxr.at[x], upx_sem.at[x], at(z, q, c))

    def upper_z():
        v = ux[x]
        for d in range(1, NX):
            q = (x + d) % NX
            arrived(uxr.at[q], upx_sem.at[q])
            v = v + uxr[q]
        uz[...] = v
        S.send(z != 0, uz, uzr.at[z], upz_sem.at[z], at(0 * z, x, c))

    def upper_last():
        @pl.when(z == 0)
        def _():
            v = uz[...]
            for q in range(1, NZ):
                arrived(uzr.at[q], upz_sem.at[q])
                v = v + uzr[q]
            uf[...] = v

        S.send((z == 0) & (x != 0), uf, ufr.at[x], upf_sem.at[x], at(z, 0 * x, c))

    upper_y()

    pl.when(x != 0)(lambda: arrived(y0b, y0_sem.at[1]))
    solved = mm_full(y0b[...], inv[...].T)
    lower_full = ls[...].astype(F32) + llo[...].astype(F32)
    change = lax.dot_general(
        solved, lower_full, (((1,), (1,)), ((), ())), precision=HIGHEST, preferred_element_type=F32
    )
    red_out[0:1, :] = targets[0:1, :] - change[0:1, :256]
    red_out[1:2, :] = targets[1:2, :] - change[0:1, 256:]

    for s in range(4):
        arrived(slot(s, xo_), ux_sem.at[2, s])
    upper_x()

    low_sum = jnp.zeros((256, 256), F32)
    whole = ut[...].reshape(2048, 256)
    for blk in range(2):
        rsl = pl.ds(blk * 256, 256)
        keep = keep_row if blk == 0 else jnp.ones((), F32)
        hi, lo = split((mm(gm[rsl, :], whole) * keep).T)
        low_sum = low_sum + mm(hi, xr[rsl, :]) + mm(lo, xr[rsl, :])
    lower = -mm_full(invt, low_sum)
    lower = lower.reshape(NZ, NX, 8, 256)
    for q in range(NX):
        lx[q] = lower[:, q]
    for d in range(1, NX):
        q = (x + d) % NX
        S.send(None, lx.at[q], lxr.at[x], lowx_sem.at[x], at(z, q, c))

    @pl.loop(0, 8)
    def _(b):
        s = pl.ds(pl.multiple_of(b * 256, 256), 256)
        u = ut[b].reshape(256, 256)
        hi, lo = split(mm(u, mh[0]) + mm(u, mh[1]))
        wc[0, s, :] = hi
        wc[1, s, :] = lo

    for blk in range(2):
        rsl = pl.ds(blk * 256, 256)
        keep = keep_row if blk == 0 else jnp.ones((), F32)
        rows = acc[rsl, :] - keep * (mm(gm[rsl, :], wc[0]) + mm(gm[rsl, :], wc[1]))
        for q in range(8):
            rb[q % 2, q // 2, blk] = rows[q * 32:(q + 1) * 32, :]
    S.send(None, rb.at[1 - k], rsib, sib_sem.at[0], sib)

    for d in range(1, NX):
        arrived(lxr.at[(x + d) % NX], lowx_sem.at[(x + d) % NX])
    lz[...] = lx[x] + lxr[xr_] + lxr[xo_] + lxr[xl_]
    for d in range(1, NZ):
        q = (z + d) % NZ
        S.send(None, lz.at[q], lzr.at[z], lowz_sem.at[z], at(q, x, c))
    upper_z()

    arrived(rsib, sib_sem.at[0])

    @pl.loop(0, 4)
    def _(q):
        v = rb[k, q] + rsib[q]
        rb[k, q] = v
        rys[q] = v.astype(BF16)

    for d in range(1, NY):
        q = (y + d) % NY
        S.send(None, rys.at[q], ryr.at[y], ry_sem.at[y], at(z, x, 2 * q + k))

    def update(b):
        u = ut[b].reshape(256, 256)
        dims = (((1,), (1,)), ((), ()))
        v = lax.dot_general(ls[...], u, dims, preferred_element_type=F32)
        v = v + lax.dot_general(llo[...], u, dims, preferred_element_type=F32)
        s = pl.ds(b, 512, stride=8)
        g32.at[0][s, :] = v[:, :128]
        g32.at[1][s, :] = v[:, 128:]

    update(0)
    update(1)

    v = lz[z]
    for d in range(1, NZ):
        q = (z + d) % NZ
        arrived(lzr.at[q], lowz_sem.at[q])
        v = v + lzr[q]
    lf[...] = v
    S.send(c != 0, lf, lfr.at[c], lowf_sem.at[c], at(z, x, 0 * c))
    upper_last()

    for b in range(2, 8):
        update(b)
    get_a.wait()
    put_a = [
        pltpu.make_async_copy(up.at[pl.ds(i * 1024, 1024)], up_out.at[pl.ds(i * 1024, 1024)], local_sem.at[4 + i])
        for i in range(4)
    ]
    for i in range(4):
        s = pl.ds(i * 1024, 1024)
        up[s, :128] = up[s, :128] - g32[0, s, :]
        up[s, 128:] = up[s, 128:] - g32[1, s, :]
        put_a[i].start()

    total = rb[k, y]
    for d in range(1, NY):
        q = (y + d) % NY
        arrived(ryr.at[q], ry_sem.at[q])
        total = total + ryr[q].astype(F32)
    rows_out[...] = total * scale

    for i in range(4):
        v = zs[z, i]
        for d in range(1, NZ):
            q = (z + d) % NZ
            arrived(zr.at[q, i], zr_sem.at[i, q])
            v = v + zr[q, i]
        cols_out[i] = v[0] * scale
        cols_out[i + 4] = v[1] * scale

    @pl.when(c == 0)
    def _():
        v = lf[...]
        for q in range(1, 8):
            arrived(lfr.at[q], lowf_sem.at[q])
            v = v + lfr[q]
        cols_out[0] = cols_out[0] + v * scale

    @pl.when((z == 0) & (x == 0))
    def _():
        rows_out[0, :8] = rows_out[0, :8] + uf[...] * scale
        for q in range(1, NX):
            arrived(ufr.at[q], upf_sem.at[q])
            rows_out[0, q * 8:(q + 1) * 8] = rows_out[0, q * 8:(q + 1) * 8] + ufr[q] * scale

    S.drain()

    @pl.loop(0, 4)
    def _(i):
        for copy in step1(i) + step2(i):
            copy.wait_send()
        for d in range(1, NZ):
            z_copy(i, d).wait_send()
    for copy in put_a:
        copy.wait()


def deliver(up, red, rows, cols, up_to, red_to, rows_to, cols_to, sems):
    copies = [
        pltpu.make_async_copy(up.at[pl.ds(i * 512, 512)], up_to.at[pl.ds(i * 512, 512)], sems.at[i]) for i in range(8)
    ] + [
        pltpu.make_async_copy(red, red_to, sems.at[8]),
        pltpu.make_async_copy(rows, rows_to, sems.at[9]),
        pltpu.make_async_copy(cols, cols_to, sems.at[10]),
    ]
    for copy in copies:
        copy.start()
    for copy in copies:
        copy.wait()


def shards(trailing, inv_block, features, targets, cot_trailing):
    tr = trailing.reshape(4096, 256)
    g = cot_trailing.reshape(4096, 256)
    feats = features.reshape(2048, 256)
    vm = pl.BlockSpec(memory_space=pltpu.VMEM)
    hbm = pl.BlockSpec(memory_space=pltpu.HBM)
    V = pltpu.VMEM
    D = pltpu.SemaphoreType.DMA
    shapes = (
        jax.ShapeDtypeStruct((4096, 256), F32),
        jax.ShapeDtypeStruct((2, 256), F32),
        jax.ShapeDtypeStruct((2, 32, 256), F32),
        jax.ShapeDtypeStruct((8, 8, 256), F32),
    )
    results = pl.pallas_call(
        comm_kernel,
        out_shape=shapes,
        in_specs=[hbm, vm, hbm, vm, hbm],
        out_specs=(hbm, vm, vm, vm),
        scratch_shapes=[
            V((4096, 256), BF16), V((2, 4096, 128), F32), V((512, 2048), BF16), V((8, 256, 512), BF16),
            V((2048, 256), BF16), V((512, 256), BF16), V((512, 256), BF16), V((512, 256), BF16),
            V((256, 256), BF16), V((8, 2, 128, 256), BF16), V((8, 256), F32), V((4096, 256), F32),
            V((2, 512, 256), BF16), V((2, 2048, 256), BF16), V((2, 256, 256), BF16), V((256, 512), BF16),
            V((4, 8, 64, 256), F32), V((8, 64, 256), BF16), V((8, 64, 256), BF16), V((8, 64, 256), BF16),
            V((8, 64, 256), BF16), V((8, 64, 256), BF16), V((8, 64, 256), BF16),
            V((8, 4, 2, 8, 256), F32), V((8, 4, 2, 8, 256), F32),
            V((2, 4, 2, 32, 256), F32), V((4, 2, 32, 256), F32), V((4, 2, 32, 256), BF16), V((4, 2, 32, 256), BF16),
            V((2, 4, 32, 256), F32), V((4, 32, 256), F32), V((4, 32, 256), F32), V((4, 32, 256), F32),
            V((4, 8, 256), F32), V((4, 8, 256), F32), V((8, 256), F32), V((8, 8, 256), F32),
            V((8, 256), F32), V((4, 8, 256), F32),
            V((4, 8, 8, 256), F32), V((4, 8, 8, 256), F32), V((8, 8, 256), F32), V((8, 8, 256), F32),
            V((8, 256), F32), V((8, 8, 256), F32),
            V((512, 256), F32),
            D((9,)), D((140,)), D((4, 4)), D((1,)), D((4,)), D((3, 4)),
            D((6, 4)), D((8,)), D((8,)), D((8,)), D((4, 8)), D((4, 8)),
            D((1,)), D((4,)), D((1,)), D((4,)), D((4,)), D((8,)), D((4,)), D((4,)), D((8,)), D((8,)), D((2,)),
        ],
        compiler_params=pltpu.CompilerParams(
            collective_id=0, has_side_effects=True, vmem_limit_bytes=63 * 1024 * 1024
        ),
        name="panel_comm",
    )(tr, inv_block, feats, targets, g)
    updated, reduced, rows, cols = pl.pallas_call(
        deliver,
        out_shape=shapes,
        in_specs=[hbm] * 4,
        out_specs=(hbm,) * 4,
        scratch_shapes=[D((11,))],
        compiler_params=pltpu.CompilerParams(vmem_limit_bytes=63 * 1024 * 1024),
        name="deliver",
    )(*results)
    return (
        updated.reshape(trailing.shape),
        reduced,
        rows.reshape(2, 1, 32, 256),
        cols.reshape(8, 1, 8, 256),
    )


def solution(mesh):
    return jax.shard_map(
        shards,
        mesh=mesh,
        in_specs=(
            P(None, "row", None, "col"),
            P(),
            P(None, "col", None, None),
            P(None, "row"),
            P(None, "row", None, "col"),
        ),
        out_specs=(
            P(None, "row", None, "col"),
            P(None, "row"),
            P(None, "row", "col", None),
            P(None, "col", "row", None),
        ),
        check_vma=False,
    )
```

```python
import functools

import jax
import jax.numpy as jnp
from jax import lax
from jax.experimental import pallas as pl
from jax.experimental.pallas import tpu as pltpu
from jax.sharding import PartitionSpec as P

MESH = pl.DeviceIdType.MESH
F32 = jnp.float32
BF16 = jnp.bfloat16
HIGHEST = lax.Precision.HIGHEST
NX, NZ, NY = 4, 8, 4


def mm(a, b):
    return jnp.dot(a, b, preferred_element_type=F32)


def split(v):
    hi = v.astype(BF16)
    return hi, (v - hi.astype(F32)).astype(BF16)


def mm_full(a, b):
    ah, al = split(a)
    bh, bl = split(b)
    return mm(ah, bh) + (mm(ah, bl) + mm(al, bh))


class Sends:
    def __init__(self, sems):
        self.sems = sems
        self.used = 0
        self.copies = []

    def make(self, src, dst, recv, device, slot=None):
        if slot is None:
            slot = self.used
            self.used += 1
        return pltpu.make_async_remote_copy(
            src_ref=src, dst_ref=dst, send_sem=self.sems.at[slot], recv_sem=recv,
            device_id=device, device_id_type=MESH,
        )

    def send(self, pred, src, dst, recv, device):
        copy = self.make(src, dst, recv, device)
        self.copies.append((pred, copy))
        if pred is None:
            copy.start()
        else:
            pl.when(pred)(copy.start)

    def drain(self):
        for pred, copy in self.copies:
            if pred is None:
                copy.wait_send()
            else:
                pl.when(pred)(copy.wait_send)


def arrived(ref, sem):
    pltpu.make_async_copy(ref, ref, sem).wait()


def comm_kernel(
    tr, inv, feats, targets, g,
    up_out, red_out, rows_out, cols_out,
    g16, g32, gm, gt, xc, ls, llo, xr, x0, ut, y0b, up,
    wr, wc, mh, lst,
    part, pm1, pright, pleft, rm1, rleft, rright, zs, zr, zf,
    rb, rsib, rys, ryr,
    ub, usib, uy, uyr, ux, uxr, uz, uzr, uf, ufr,
    lx, lxr, lxf, lz, lzr, lf, lfr,
    acc,
    local_sem, send_sem, s1_sem, ua_sem, uz_sem, ux_sem,
    cs_sem, m1_sem, m2l_sem, m2r_sem, zss_sem, zr_sem,
    sib_sem, ry_sem, up_sem, upy_sem, upx_sem, upz_sem, upf_sem, lowx_sem, lowz_sem, lowf_sem, y0_sem,
):
    r = lax.axis_index("row")
    c = lax.axis_index("col")
    z, x = r // NX, r % NX
    y, k = c // 2, c % 2
    xr_, xl_, xo_ = (x + 1) % NX, (x + 3) % NX, (x + 2) % NX

    def at(z_, x_, c_):
        return (z_ * NX + x_, c_)

    sib = at(z, x, 2 * y + 1 - k)
    S = Sends(send_sem)
    scale = 1.0 / feats.shape[1]

    get_g = pltpu.make_async_copy(g, g16, local_sem.at[0])
    get_f = pltpu.make_async_copy(feats, xc, local_sem.at[1])
    get_t = [pltpu.make_async_copy(tr.at[:, pl.ds(h * 128, 128)], g32.at[h], local_sem.at[2 + 6 * h]) for h in range(2)]

    @pl.when(c == 0)
    def _():
        get_t[0].start()
        get_t[1].start()

    get_f.start()
    get_a = pltpu.make_async_copy(tr, up, local_sem.at[3])

    @pl.when(c != 0)
    def _():
        get_g.start()
        get_a.start()

    def by_stride(b):
        s = pl.ds(b, 512, stride=8)
        return jnp.concatenate([g32.at[0][s, :], g32.at[1][s, :]], axis=1)

    bar = pltpu.get_barrier_semaphore()
    pl.semaphore_signal(bar, inc=1, device_id=sib, device_id_type=MESH)
    for d in range(1, NY):
        pl.semaphore_signal(bar, inc=1, device_id=at(z, x, 2 * ((y + d) % NY) + k), device_id_type=MESH)
    for d in range(1, NX):
        pl.semaphore_signal(bar, inc=1, device_id=at(z, (x + d) % NX, c), device_id_type=MESH)
    for d in range(1, NZ):
        pl.semaphore_signal(bar, inc=1, device_id=at((z + d) % NZ, x, c), device_id_type=MESH)
    srow = (z % 2) == (c // 4)
    home = c % 4
    cr = r % 8

    @pl.when(srow & jnp.logical_not((c == 0) & (x == home)))
    def _():
        pl.semaphore_signal(bar, inc=1, device_id=at(z, home, 0 * c), device_id_type=MESH)

    @pl.when(c == 0)
    def _():
        for q in (3, 5, 7):
            pl.semaphore_signal(bar, inc=1, device_id=at(z, x, q), device_id_type=MESH)

    @pl.when(c == 0)
    def _():
        get_t[0].wait()
        get_t[1].wait()
        low = mm_full(by_stride(0), inv[...].T)
        keep = jnp.where((r == 0) & (lax.broadcasted_iota(jnp.int32, (512, 256), 0) < 256), 0.0, 1.0)
        hi, lo = split(low * keep.astype(F32))
        ls[...] = hi
        llo[...] = lo

    pl.semaphore_wait(
        bar, 14 + jnp.where(c == 0, 4 - jnp.where(cr == 0, 1, 0), 0) + jnp.where((k == 1) & (c >= 3), 1, 0)
    )

    keep_row = jnp.where(r == 0, 0.0, 1.0).astype(F32)
    keep_col = jnp.where(c == 0, 0.0, 1.0).astype(F32)

    def piece(ref, q):
        n = ref.shape[0] // NY
        return ref.at[pl.ds(pl.multiple_of(q * n, n), n)]

    def bcast_root(ref, which, yr, kr):
        root = (y == yr) & (k == kr)
        sems = s1_sem.at[which]
        for d in range(1, NY):
            q = (yr + d) % NY
            S.send(root, piece(ref, q), piece(ref, q), sems.at[d], at(z, x, 2 * q + kr))
        for d in range(1, NY):
            q = (yr + d) % NY
            S.send(root, piece(ref, yr), piece(ref, yr), sems.at[0], at(z, x, 2 * q + kr))
        for d in range(NY):
            q = (yr + d) % NY
            S.send(root, piece(ref, q), piece(ref, q), sems.at[d], sib)

    def bcast_own(ref, which, yr, kr):
        relay = (y != yr) & (k == kr)
        sems = s1_sem.at[which]
        d0 = (y - yr + NY) % NY
        mine = piece(ref, y)
        pl.when(relay)(lambda: arrived(mine, sems.at[d0]))
        for e in (d0 % 3 + 1, (d0 + 1) % 3 + 1):
            S.send(relay, mine, mine, sems.at[d0], at(z, x, 2 * ((yr + e) % NY) + kr))
        S.send(relay, mine, mine, sems.at[d0], sib)

    def bcast_rest(ref, which, yr, kr):
        relay = (y != yr) & (k == kr)
        sems = s1_sem.at[which]
        d0 = (y - yr + NY) % NY
        for e in (d0 * 0, d0 % 3 + 1, (d0 + 1) % 3 + 1):
            p = piece(ref, (yr + e) % NY)
            pl.when(relay)(functools.partial(arrived, p, sems.at[e]))
            S.send(relay, p, p, sems.at[e], sib)

    def bcast_end(ref, which, yr, kr):
        @pl.when(k != kr)
        def _():
            for e in range(NY):
                arrived(piece(ref, (yr + e) % NY), s1_sem.at[which].at[e])

    yr2, kr2 = cr // 2, cr % 2
    b0 = r // 8
    mys = z // 2

    def slot(s, x_):
        return ut.at[s + 4 * (x_ // 2), x_ % 2]

    for q in range(NX):
        mine = (cr == 0) & (x == q)
        chunk = ls.at[pl.ds(q * 128, 128)]
        S.send((c == 0) & jnp.logical_not(mine), chunk, slot(mys, q), ua_sem.at[0], at(z, q, cr))

        @pl.when((c == 0) & mine)
        def _():
            ut[mys + 4 * (q // 2), q % 2] = chunk[...]

    bcast_root(ls, 0, 0, 0)
    get_f.wait()

    @pl.when(c == 0)
    def _():
        get_g.start()
        get_a.start()
        x0[...] = xc[pl.ds(0, 256), :]

    bcast_root(x0, 1, 0, 0)

    @pl.when(c == cr)
    def _():
        xr[pl.ds(0, 256), :] = xc[pl.ds(pl.multiple_of(b0 * 256, 256), 256), :]
        xr[pl.ds(256, 256), :] = xc[pl.ds(pl.multiple_of(b0 * 256 + 1024, 256), 256), :]

    bcast_root(xr, 2, yr2, kr2)

    first = (z == 0) & (x == 0)

    @pl.when(first)
    def _():
        y0b[...] = jnp.broadcast_to(targets[0:1, :], (8, 256))

    for d in range(1, NZ):
        S.send(first, y0b, y0b, y0_sem.at[0], at((z + d) % NZ, x, c))

    def relayout(b):
        v = by_stride(b).astype(BF16)
        gm[:, b * 256:(b + 1) * 256] = v
        gt[b] = v.T

    get_g.wait()

    @pl.loop(0, 8)
    def _(i):
        s = pl.ds(pl.multiple_of(i * 512, 512), 512)
        v = g16[s, :].astype(F32)
        g32[0, s, :] = v[:, :128]
        g32[1, s, :] = v[:, 128:]

    right, left_ = at(z, xr_, c), at(z, xl_, c)
    far_s = [((z + jnp.where(srow, near, off) + NZ) % NZ) // 2 for near, off in ((0, -1), (2, 1), (-2, 3), (4, -3))]

    def forward_upper(n):
        p = slot(far_s[n], x)
        if n == 0:
            pl.when(jnp.logical_not(srow))(lambda: arrived(p, uz_sem.at[far_s[0]]))
        else:
            arrived(p, uz_sem.at[far_s[n]])
        S.send(None, p, p, ux_sem.at[0, far_s[n]], right)
        S.send(None, p, p, ux_sem.at[1, far_s[n]], left_)

    own = slot(mys, x)
    pl.when(srow & jnp.logical_not((c == 0) & (x == home)))(lambda: arrived(own, ua_sem.at[0]))
    for d in (4, 3, 5, 2, 6, 1, 7):
        S.send(srow, own, own, uz_sem.at[mys], at((z + d) % NZ, x, c))
    bcast_own(ls, 0, 0, 0)
    bcast_own(x0, 1, 0, 0)
    bcast_own(xr, 2, yr2, kr2)
    forward_upper(0)
    relayout(0)
    relayout(1)
    bcast_rest(ls, 0, 0, 0)
    forward_upper(1)
    bcast_rest(x0, 1, 0, 0)
    bcast_rest(xr, 2, yr2, kr2)
    relayout(2)
    relayout(3)
    forward_upper(2)
    relayout(4)
    relayout(5)
    forward_upper(3)
    relayout(6)
    relayout(7)
    bcast_end(ls, 0, 0, 0)
    bcast_end(x0, 1, 0, 0)
    bcast_end(xr, 2, yr2, kr2)

    bcast_root(llo, 3, 0, 0)

    pl.when((x == 0) & (z != 0))(lambda: arrived(y0b, y0_sem.at[0]))
    for d in range(1, NX):
        S.send(x == 0, y0b, y0b, y0_sem.at[1], at(z, (x + d) % NX, c))

    mapped = mm_full(inv[...], x0[...].astype(F32))
    hi, lo = split(mapped)
    mh[0] = hi
    mh[1] = lo
    lst[...] = ls[...].T
    hi, lo = split(mm(ls[...], mh[0]) + mm(ls[...], mh[1]))
    wr[0] = hi
    wr[1] = lo

    def cols_block(b):
        keep = jnp.where((c == 0) & (b == 0), 0.0, 1.0).astype(F32)
        left = gt[b]
        v = mm(left, xr[...]) - keep * (mm(left, wr[0]) + mm(left, wr[1]))
        v = v.reshape(NZ, NX, 8, 256)
        for q in range(NX):
            part[q, b] = v[:, q].reshape(64, 256)

    def x_copy(src, dst, recv, which, i, device):
        return pltpu.make_async_remote_copy(
            src_ref=src, dst_ref=dst, send_sem=cs_sem.at[which, i], recv_sem=recv,
            device_id=device, device_id_type=MESH,
        )

    def step1(i):
        j = i + 4
        return (
            x_copy(pm1.at[i], rm1.at[i], m1_sem.at[i], 0, i, right),
            x_copy(pleft.at[i], rright.at[i], m2r_sem.at[i], 1, i, left_),
            x_copy(pm1.at[j], rm1.at[j], m1_sem.at[j], 2, i, left_),
            x_copy(pright.at[j], rleft.at[j], m2l_sem.at[j], 3, i, right),
        )

    def step2(i):
        j = i + 4
        return (
            x_copy(pright.at[i], rleft.at[i], m2l_sem.at[i], 4, i, right),
            x_copy(pleft.at[j], rright.at[j], m2r_sem.at[j], 5, i, left_),
        )

    def cols_step(i):
        cols_block(i)
        cols_block(i + 4)
        j = i + 4
        pm1[i] = part[xo_, i].astype(BF16)
        pleft[i] = part[xl_, i].astype(BF16)
        pm1[j] = part[xo_, j].astype(BF16)
        pright[j] = part[xr_, j].astype(BF16)
        for copy in step1(i):
            copy.start()

    def relay_upper(s):
        p = slot(s, xl_)
        arrived(p, ux_sem.at[0, s])
        S.send(s < 2, p, p, ux_sem.at[2, s], right)
        p = slot(s, xr_)
        arrived(p, ux_sem.at[1, s])
        S.send(s >= 2, p, p, ux_sem.at[2, s], left_)

    pl.loop(0, 2)(cols_step)
    relay_upper(far_s[0])
    relay_upper(far_s[1])
    pl.loop(2, 4)(cols_step)
    relay_upper(far_s[2])
    relay_upper(far_s[3])

    @pl.loop(0, 4)
    def _(i):
        j = i + 4
        arrived(rm1.at[i], m1_sem.at[i])
        pright[i] = (part[xr_, i] + rm1[i].astype(F32)).astype(BF16)
        arrived(rm1.at[j], m1_sem.at[j])
        pleft[j] = (part[xl_, j] + rm1[j].astype(F32)).astype(BF16)
        for copy in step2(i):
            copy.start()

    bcast_own(llo, 3, 0, 0)

    for blk in range(2):
        rsl = pl.ds(blk * 256, 256)
        first_col = mm(gm[rsl, :256], xc[:256, :])
        rest = mm(gm[rsl, 256:], xc[256:, :])
        acc[rsl, :] = rest + first_col
        hi, lo = split(rest + keep_col * first_col)
        wc[0, rsl, :] = hi
        wc[1, rsl, :] = lo
    upper = mm(lst[...], wc[0, :512, :]) + mm(lst[...], wc[1, :512, :])
    invt = inv[...].T
    upper = -mm_full(invt, upper)
    for q in range(8):
        ub[q % 2, q // 2] = upper[q * 32:(q + 1) * 32, :]
    S.send(None, ub.at[1 - k], usib, up_sem.at[0], sib)

    def upper_y():
        arrived(usib, up_sem.at[0])
        uy[...] = ub[k] + usib[...]
        for d in range(1, NY):
            q = (y + d) % NY
            S.send(None, uy.at[q], uyr.at[y], upy_sem.at[y], at(z, x, 2 * q + k))

    def upper_x():
        v = uy[y]
        for d in range(1, NY):
            q = (y + d) % NY
            arrived(uyr.at[q], upy_sem.at[q])
            v = v + uyr[q]
        for q in range(NX):
            ux[q] = v[q * 8:(q + 1) * 8]
        for d in range(1, NX):
            q = (x + d) % NX
            S.send(None, ux.at[q], uxr.at[x], upx_sem.at[x], at(z, q, c))

    def upper_z():
        v = ux[x]
        for d in range(1, NX):
            q = (x + d) % NX
            arrived(uxr.at[q], upx_sem.at[q])
            v = v + uxr[q]
        uz[...] = v
        S.send(z != 0, uz, uzr.at[z], upz_sem.at[z], at(0 * z, x, c))

    def upper_last():
        @pl.when(z == 0)
        def _():
            v = uz[...]
            for q in range(1, NZ):
                arrived(uzr.at[q], upz_sem.at[q])
                v = v + uzr[q]
            uf[...] = v

        S.send((z == 0) & (x != 0), uf, ufr.at[x], upf_sem.at[x], at(z, 0 * x, c))

    for s in range(4):
        arrived(slot(s, xo_), ux_sem.at[2, s])
    low_sum = jnp.zeros((256, 256), F32)
    whole = ut[...].reshape(2048, 256)
    for blk in range(2):
        rsl = pl.ds(blk * 256, 256)
        keep = keep_row if blk == 0 else jnp.ones((), F32)
        hi, lo = split((mm(gm[rsl, :], whole) * keep).T)
        low_sum = low_sum + mm(hi, xr[rsl, :]) + mm(lo, xr[rsl, :])
    lower = -mm_full(invt, low_sum)
    lower = lower.reshape(NZ, NX, 8, 256)
    for q in range(NX):
        lx[q] = lower[:, q].reshape(64, 256).astype(BF16)
        lxf[q] = lower[:, q].reshape(64, 256)
    for d in range(1, NX):
        q = (x + d) % NX
        S.send(None, lx.at[q], lxr.at[x], lowx_sem.at[x], at(z, q, c))

    def z_copy(i, d):
        zd = (z + d) % NZ
        return pltpu.make_async_remote_copy(
            src_ref=zs.at[zd, i], dst_ref=zr.at[z, i], send_sem=zss_sem.at[i, d], recv_sem=zr_sem.at[i, z],
            device_id=at(zd, x, c), device_id_type=MESH,
        )

    @pl.loop(0, 4)
    def _(i):
        for h in range(2):
            b = i + 4 * h
            arrived(rleft.at[b], m2l_sem.at[b])
            arrived(rright.at[b], m2r_sem.at[b])
            v = part[x, b] + rleft[b].astype(F32) + rright[b].astype(F32)
            v = v.reshape(NZ, 8, 256)
            zf[i, h] = v
            for q in range(NZ):
                zs[q, i, h] = v[q].astype(BF16)
        for d in range(1, NZ):
            z_copy(i, d).start()

    bcast_rest(llo, 3, 0, 0)
    upper_y()

    @pl.loop(0, 8)
    def _(b):
        s = pl.ds(pl.multiple_of(b * 256, 256), 256)
        u = ut[b].reshape(256, 256)
        hi, lo = split(mm(u, mh[0]) + mm(u, mh[1]))
        wc[0, s, :] = hi
        wc[1, s, :] = lo

    for blk in range(2):
        rsl = pl.ds(blk * 256, 256)
        keep = keep_row if blk == 0 else jnp.ones((), F32)
        rows = acc[rsl, :] - keep * (mm(gm[rsl, :], wc[0]) + mm(gm[rsl, :], wc[1]))
        for q in range(8):
            rb[q % 2, q // 2, blk] = rows[q * 32:(q + 1) * 32, :]
    S.send(None, rb.at[1 - k], rsib, sib_sem.at[0], sib)

    for d in range(1, NX):
        arrived(lxr.at[(x + d) % NX], lowx_sem.at[(x + d) % NX])
    v = lxf[x] + lxr[xr_].astype(F32) + lxr[xo_].astype(F32) + lxr[xl_].astype(F32)
    lz[...] = v.reshape(NZ, 8, 256)
    for d in range(1, NZ):
        q = (z + d) % NZ
        S.send(None, lz.at[q], lzr.at[z], lowz_sem.at[z], at(q, x, c))
    upper_x()

    arrived(rsib, sib_sem.at[0])

    @pl.loop(0, 4)
    def _(q):
        v = rb[k, q] + rsib[q]
        rb[k, q] = v
        rys[q] = v.astype(BF16)

    for d in range(1, NY):
        q = (y + d) % NY
        S.send(None, rys.at[q], ryr.at[y], ry_sem.at[y], at(z, x, 2 * q + k))

    def update(b):
        u = ut[b].reshape(256, 256)
        dims = (((1,), (1,)), ((), ()))
        v = lax.dot_general(ls[...], u, dims, preferred_element_type=F32)
        v = v + lax.dot_general(llo[...], u, dims, preferred_element_type=F32)
        s = pl.ds(b, 512, stride=8)
        g32.at[0][s, :] = v[:, :128]
        g32.at[1][s, :] = v[:, 128:]

    bcast_end(llo, 3, 0, 0)
    update(0)
    update(1)
    upper_z()

    v = lz[z]
    for d in range(1, NZ):
        q = (z + d) % NZ
        arrived(lzr.at[q], lowz_sem.at[q])
        v = v + lzr[q]
    lf[...] = v
    S.send(c != 0, lf, lfr.at[c], lowf_sem.at[c], at(z, x, 0 * c))
    update(2)
    update(3)
    upper_last()
    pl.when(x != 0)(lambda: arrived(y0b, y0_sem.at[1]))
    solved = mm_full(y0b[...], inv[...].T)
    lower_full = ls[...].astype(F32) + llo[...].astype(F32)
    change = lax.dot_general(
        solved, lower_full, (((1,), (1,)), ((), ())), precision=HIGHEST, preferred_element_type=F32
    )
    red_out[0:1, :] = targets[0:1, :] - change[0:1, :256]
    red_out[1:2, :] = targets[1:2, :] - change[0:1, 256:]

    for b in range(4, 8):
        update(b)
    get_a.wait()
    put_a = [
        pltpu.make_async_copy(up.at[pl.ds(i * 1024, 1024)], up_out.at[pl.ds(i * 1024, 1024)], local_sem.at[4 + i])
        for i in range(4)
    ]
    for i in range(4):
        s = pl.ds(i * 1024, 1024)
        up[s, :128] = up[s, :128] - g32[0, s, :]
        up[s, 128:] = up[s, 128:] - g32[1, s, :]
        put_a[i].start()

    total = rb[k, y]
    for d in range(1, NY):
        q = (y + d) % NY
        arrived(ryr.at[q], ry_sem.at[q])
        total = total + ryr[q].astype(F32)
    rows_out[...] = total * scale

    for i in range(4):
        v = [zf[i, h, z] for h in range(2)]
        for d in range(1, NZ):
            q = (z + d) % NZ
            arrived(zr.at[q, i], zr_sem.at[i, q])
            for h in range(2):
                v[h] = v[h] + zr[q, i, h].astype(F32)
        cols_out[i] = v[0] * scale
        cols_out[i + 4] = v[1] * scale

    @pl.when(c == 0)
    def _():
        v = lf[...]
        for q in range(1, 8):
            arrived(lfr.at[q], lowf_sem.at[q])
            v = v + lfr[q]
        cols_out[0] = cols_out[0] + v * scale

    @pl.when((z == 0) & (x == 0))
    def _():
        rows_out[0, :8] = rows_out[0, :8] + uf[...] * scale
        for q in range(1, NX):
            arrived(ufr.at[q], upf_sem.at[q])
            rows_out[0, q * 8:(q + 1) * 8] = rows_out[0, q * 8:(q + 1) * 8] + ufr[q] * scale

    S.drain()

    @pl.loop(0, 4)
    def _(i):
        for copy in step1(i) + step2(i):
            copy.wait_send()
        for d in range(1, NZ):
            z_copy(i, d).wait_send()
    for copy in put_a:
        copy.wait()


def deliver(up, red, rows, cols, up_to, red_to, rows_to, cols_to, upv, redv, rowsv, colsv, sems):
    def part(ref, i):
        return ref.at[pl.ds(i * 512, 512)]

    pairs = [(part(up, i), part(upv, i), part(up_to, i)) for i in range(8)]
    pairs += [(red, redv, red_to), (rows, rowsv, rows_to), (cols, colsv, cols_to)]
    take = [pltpu.make_async_copy(src, mid, sems.at[0, i]) for i, (src, mid, _) in enumerate(pairs)]
    give = [pltpu.make_async_copy(mid, dst, sems.at[1, i]) for i, (_, mid, dst) in enumerate(pairs)]
    for copy in take:
        copy.start()
    for i in range(len(pairs)):
        take[i].wait()
        give[i].start()
    for copy in give:
        copy.wait()


def shards(trailing, inv_block, features, targets, cot_trailing):
    tr = trailing.reshape(4096, 256)
    g = cot_trailing.reshape(4096, 256)
    feats = features.reshape(2048, 256)
    vm = pl.BlockSpec(memory_space=pltpu.VMEM)
    hbm = pl.BlockSpec(memory_space=pltpu.HBM)
    V = pltpu.VMEM
    D = pltpu.SemaphoreType.DMA
    shapes = (
        jax.ShapeDtypeStruct((4096, 256), F32),
        jax.ShapeDtypeStruct((2, 256), F32),
        jax.ShapeDtypeStruct((2, 32, 256), F32),
        jax.ShapeDtypeStruct((8, 8, 256), F32),
    )
    results = pl.pallas_call(
        comm_kernel,
        out_shape=shapes,
        in_specs=[hbm, vm, hbm, vm, hbm],
        out_specs=(hbm, vm, vm, vm),
        scratch_shapes=[
            V((4096, 256), BF16), V((2, 4096, 128), F32), V((512, 2048), BF16), V((8, 256, 512), BF16),
            V((2048, 256), BF16), V((512, 256), BF16), V((512, 256), BF16), V((512, 256), BF16),
            V((256, 256), BF16), V((8, 2, 128, 256), BF16), V((8, 256), F32), V((4096, 256), F32),
            V((2, 512, 256), BF16), V((2, 2048, 256), BF16), V((2, 256, 256), BF16), V((256, 512), BF16),
            V((4, 8, 64, 256), F32), V((8, 64, 256), BF16), V((8, 64, 256), BF16), V((8, 64, 256), BF16),
            V((8, 64, 256), BF16), V((8, 64, 256), BF16), V((8, 64, 256), BF16),
            V((8, 4, 2, 8, 256), BF16), V((8, 4, 2, 8, 256), BF16), V((4, 2, 8, 8, 256), F32),
            V((2, 4, 2, 32, 256), F32), V((4, 2, 32, 256), F32), V((4, 2, 32, 256), BF16), V((4, 2, 32, 256), BF16),
            V((2, 4, 32, 256), F32), V((4, 32, 256), F32), V((4, 32, 256), F32), V((4, 32, 256), F32),
            V((4, 8, 256), F32), V((4, 8, 256), F32), V((8, 256), F32), V((8, 8, 256), F32),
            V((8, 256), F32), V((4, 8, 256), F32),
            V((4, 64, 256), BF16), V((4, 64, 256), BF16), V((4, 64, 256), F32), V((8, 8, 256), F32), V((8, 8, 256), F32),
            V((8, 256), F32), V((8, 8, 256), F32),
            V((512, 256), F32),
            D((9,)), D((140,)), D((4, 4)), D((1,)), D((4,)), D((3, 4)),
            D((6, 4)), D((8,)), D((8,)), D((8,)), D((4, 8)), D((4, 8)),
            D((1,)), D((4,)), D((1,)), D((4,)), D((4,)), D((8,)), D((4,)), D((4,)), D((8,)), D((8,)), D((2,)),
        ],
        compiler_params=pltpu.CompilerParams(
            collective_id=0, has_side_effects=True, vmem_limit_bytes=63 * 1024 * 1024
        ),
        name="panel_comm",
    )(tr, inv_block, feats, targets, g)
    updated, reduced, rows, cols = pl.pallas_call(
        deliver,
        out_shape=shapes,
        in_specs=[hbm] * 4,
        out_specs=(hbm,) * 4,
        scratch_shapes=[V(v.shape, v.dtype) for v in shapes] + [D((2, 11))],
        compiler_params=pltpu.CompilerParams(vmem_limit_bytes=63 * 1024 * 1024),
        name="deliver",
    )(*results)
    return (
        updated.reshape(trailing.shape),
        reduced,
        rows.reshape(2, 1, 32, 256),
        cols.reshape(8, 1, 8, 256),
    )


def solution(mesh):
    return jax.shard_map(
        shards,
        mesh=mesh,
        in_specs=(
            P(None, "row", None, "col"),
            P(),
            P(None, "col", None, None),
            P(None, "row"),
            P(None, "row", None, "col"),
        ),
        out_specs=(
            P(None, "row", None, "col"),
            P(None, "row"),
            P(None, "row", "col", None),
            P(None, "col", "row", None),
        ),
        check_vma=False,
    )
```

```python
import functools

import jax
import jax.numpy as jnp
from jax import lax
from jax.experimental import pallas as pl
from jax.experimental.pallas import tpu as pltpu
from jax.sharding import PartitionSpec as P

MESH = pl.DeviceIdType.MESH
F32 = jnp.float32
BF16 = jnp.bfloat16
HIGHEST = lax.Precision.HIGHEST
NX, NZ, NY = 4, 8, 4


def mm(a, b):
    return jnp.dot(a, b, preferred_element_type=F32)


def split(v):
    hi = v.astype(BF16)
    return hi, (v - hi.astype(F32)).astype(BF16)


def mm_full(a, b):
    ah, al = split(a)
    bh, bl = split(b)
    return mm(ah, bh) + (mm(ah, bl) + mm(al, bh))


class Sends:
    def __init__(self, sems):
        self.sems = sems
        self.used = 0
        self.copies = []

    def make(self, src, dst, recv, device, slot=None):
        if slot is None:
            slot = self.used
            self.used += 1
        return pltpu.make_async_remote_copy(
            src_ref=src, dst_ref=dst, send_sem=self.sems.at[slot], recv_sem=recv,
            device_id=device, device_id_type=MESH,
        )

    def send(self, pred, src, dst, recv, device):
        copy = self.make(src, dst, recv, device)
        self.copies.append((pred, copy))
        if pred is None:
            copy.start()
        else:
            pl.when(pred)(copy.start)

    def drain(self):
        for pred, copy in self.copies:
            if pred is None:
                copy.wait_send()
            else:
                pl.when(pred)(copy.wait_send)


def arrived(ref, sem):
    pltpu.make_async_copy(ref, ref, sem).wait()


def comm_kernel(
    tr, inv, feats, targets, g,
    up_out, red_out, rows_out, cols_out,
    g16, g32, gm, gt, xc, ls, llo, xr, x0, ut, y0b, up,
    wr, wc, mh, lst,
    part, pm1, pright, pleft, rm1, rleft, rright, zs, zr, zf,
    rb, rsib, rys, ryr,
    ub, usib, uy, uyr, uz, uzr, uf, ufr,
    lx, lxr, lxf, lz, lzr, lf, lfr,
    acc,
    local_sem, send_sem, s1_sem, ua_sem, uz_sem, ux_sem,
    cs_sem, m1_sem, m2l_sem, m2r_sem, zss_sem, zr_sem,
    sib_sem, ry_sem, up_sem, upy_sem, upz_sem, upf_sem, lowx_sem, lowz_sem, lowf_sem, y0_sem,
):
    r = lax.axis_index("row")
    c = lax.axis_index("col")
    z, x = r // NX, r % NX
    y, k = c // 2, c % 2
    xr_, xl_, xo_ = (x + 1) % NX, (x + 3) % NX, (x + 2) % NX

    def at(z_, x_, c_):
        return (z_ * NX + x_, c_)

    sib = at(z, x, 2 * y + 1 - k)
    S = Sends(send_sem)
    scale = 1.0 / feats.shape[1]

    get_g = pltpu.make_async_copy(g, g16, local_sem.at[0])
    get_f = pltpu.make_async_copy(feats, xc, local_sem.at[1])
    get_t = [pltpu.make_async_copy(tr.at[:, pl.ds(h * 128, 128)], g32.at[h], local_sem.at[2 + 6 * h]) for h in range(2)]

    @pl.when(c == 0)
    def _():
        get_t[0].start()
        get_t[1].start()

    get_f.start()
    get_a = pltpu.make_async_copy(tr, up, local_sem.at[3])

    @pl.when(c != 0)
    def _():
        get_g.start()
        get_a.start()

    def by_stride(b):
        s = pl.ds(b, 512, stride=8)
        return jnp.concatenate([g32.at[0][s, :], g32.at[1][s, :]], axis=1)

    bar = pltpu.get_barrier_semaphore()
    pl.semaphore_signal(bar, inc=1, device_id=sib, device_id_type=MESH)
    for d in range(1, NY):
        pl.semaphore_signal(bar, inc=1, device_id=at(z, x, 2 * ((y + d) % NY) + k), device_id_type=MESH)
    for d in range(1, NX):
        pl.semaphore_signal(bar, inc=1, device_id=at(z, (x + d) % NX, c), device_id_type=MESH)
    for d in range(1, NZ):
        pl.semaphore_signal(bar, inc=1, device_id=at((z + d) % NZ, x, c), device_id_type=MESH)
    srow = (z % 2) == (c // 4)
    home = c % 4
    cr = r % 8

    @pl.when(srow & jnp.logical_not((c == 0) & (x == home)))
    def _():
        pl.semaphore_signal(bar, inc=1, device_id=at(z, home, 0 * c), device_id_type=MESH)

    @pl.when(c == 0)
    def _():
        for q in (3, 5, 7):
            pl.semaphore_signal(bar, inc=1, device_id=at(z, x, q), device_id_type=MESH)

    @pl.when(c == 0)
    def _():
        get_t[0].wait()
        get_t[1].wait()
        low = mm_full(by_stride(0), inv[...].T)
        keep = jnp.where((r == 0) & (lax.broadcasted_iota(jnp.int32, (512, 256), 0) < 256), 0.0, 1.0)
        hi, lo = split(low * keep.astype(F32))
        ls[...] = hi
        llo[...] = lo

    pl.semaphore_wait(
        bar, 14 + jnp.where(c == 0, 4 - jnp.where(cr == 0, 1, 0), 0) + jnp.where((k == 1) & (c >= 3), 1, 0)
    )

    keep_row = jnp.where(r == 0, 0.0, 1.0).astype(F32)
    keep_col = jnp.where(c == 0, 0.0, 1.0).astype(F32)

    def piece(ref, q):
        n = ref.shape[0] // NY
        return ref.at[pl.ds(pl.multiple_of(q * n, n), n)]

    def bcast_root(ref, which, yr, kr):
        root = (y == yr) & (k == kr)
        sems = s1_sem.at[which]
        for d in range(1, NY):
            q = (yr + d) % NY
            S.send(root, piece(ref, q), piece(ref, q), sems.at[d], at(z, x, 2 * q + kr))
        for d in range(1, NY):
            q = (yr + d) % NY
            S.send(root, piece(ref, yr), piece(ref, yr), sems.at[0], at(z, x, 2 * q + kr))
        for d in range(NY):
            q = (yr + d) % NY
            S.send(root, piece(ref, q), piece(ref, q), sems.at[d], sib)

    def bcast_own(ref, which, yr, kr):
        relay = (y != yr) & (k == kr)
        sems = s1_sem.at[which]
        d0 = (y - yr + NY) % NY
        mine = piece(ref, y)
        pl.when(relay)(lambda: arrived(mine, sems.at[d0]))
        for e in (d0 % 3 + 1, (d0 + 1) % 3 + 1):
            S.send(relay, mine, mine, sems.at[d0], at(z, x, 2 * ((yr + e) % NY) + kr))
        S.send(relay, mine, mine, sems.at[d0], sib)

    def bcast_rest(ref, which, yr, kr):
        relay = (y != yr) & (k == kr)
        sems = s1_sem.at[which]
        d0 = (y - yr + NY) % NY
        for e in (d0 * 0, d0 % 3 + 1, (d0 + 1) % 3 + 1):
            p = piece(ref, (yr + e) % NY)
            pl.when(relay)(functools.partial(arrived, p, sems.at[e]))
            S.send(relay, p, p, sems.at[e], sib)

    def bcast_end(ref, which, yr, kr):
        @pl.when(k != kr)
        def _():
            for e in range(NY):
                arrived(piece(ref, (yr + e) % NY), s1_sem.at[which].at[e])

    yr2, kr2 = cr // 2, cr % 2
    b0 = r // 8
    mys = z // 2

    def slot(s, x_):
        return ut.at[s + 4 * (x_ // 2), x_ % 2]

    for q in range(NX):
        mine = (cr == 0) & (x == q)
        chunk = ls.at[pl.ds(q * 128, 128)]
        S.send((c == 0) & jnp.logical_not(mine), chunk, slot(mys, q), ua_sem.at[0], at(z, q, cr))

        @pl.when((c == 0) & mine)
        def _():
            ut[mys + 4 * (q // 2), q % 2] = chunk[...]

    bcast_root(ls, 0, 0, 0)
    get_f.wait()

    @pl.when(c == 0)
    def _():
        get_g.start()
        get_a.start()
        x0[...] = xc[pl.ds(0, 256), :]

    bcast_root(x0, 1, 0, 0)

    @pl.when(c == cr)
    def _():
        xr[pl.ds(0, 256), :] = xc[pl.ds(pl.multiple_of(b0 * 256, 256), 256), :]
        xr[pl.ds(256, 256), :] = xc[pl.ds(pl.multiple_of(b0 * 256 + 1024, 256), 256), :]

    bcast_root(xr, 2, yr2, kr2)

    first = (z == 0) & (x == 0)

    @pl.when(first)
    def _():
        y0b[...] = jnp.broadcast_to(targets[0:1, :], (8, 256))

    for d in range(1, NZ):
        S.send(first, y0b, y0b, y0_sem.at[0], at((z + d) % NZ, x, c))

    def relayout(b):
        v = by_stride(b).astype(BF16)
        gm[:, b * 256:(b + 1) * 256] = v
        gt[b] = v.T

    get_g.wait()

    @pl.loop(0, 8)
    def _(i):
        s = pl.ds(pl.multiple_of(i * 512, 512), 512)
        v = g16[s, :].astype(F32)
        g32[0, s, :] = v[:, :128]
        g32[1, s, :] = v[:, 128:]

    right, left_ = at(z, xr_, c), at(z, xl_, c)
    far_s = [((z + jnp.where(srow, near, off) + NZ) % NZ) // 2 for near, off in ((0, -1), (2, 1), (-2, 3), (4, -3))]

    def forward_upper(n):
        p = slot(far_s[n], x)
        if n == 0:
            pl.when(jnp.logical_not(srow))(lambda: arrived(p, uz_sem.at[far_s[0]]))
        else:
            arrived(p, uz_sem.at[far_s[n]])
        if n >= 2:
            step = 7 if n == 2 else 1
            hp = ut.at[far_s[n] + 4 * (x // 2), x % 2, pl.ds(64 * (n - 2), 64)]
            S.send(jnp.logical_not(srow), hp, hp, uz_sem.at[far_s[n]], at((z + step) % NZ, x, c))
        S.send(None, p, p, ux_sem.at[0, far_s[n]], right)
        S.send(None, p, p, ux_sem.at[1, far_s[n]], left_)

    own = slot(mys, x)
    pl.when(srow & jnp.logical_not((c == 0) & (x == home)))(lambda: arrived(own, ua_sem.at[0]))
    for d in (1, 7, 2, 6, 3, 5):
        S.send(srow, own, own, uz_sem.at[mys], at((z + d) % NZ, x, c))
    bcast_own(ls, 0, 0, 0)
    bcast_own(x0, 1, 0, 0)
    bcast_own(xr, 2, yr2, kr2)
    forward_upper(0)
    relayout(0)
    relayout(1)
    forward_upper(1)
    bcast_rest(ls, 0, 0, 0)
    bcast_rest(x0, 1, 0, 0)
    bcast_rest(xr, 2, yr2, kr2)
    relayout(2)
    relayout(3)
    forward_upper(2)
    relayout(4)
    relayout(5)
    forward_upper(3)
    relayout(6)
    relayout(7)
    bcast_end(ls, 0, 0, 0)
    bcast_end(x0, 1, 0, 0)
    bcast_end(xr, 2, yr2, kr2)

    bcast_root(llo, 3, 0, 0)

    pl.when((x == 0) & (z != 0))(lambda: arrived(y0b, y0_sem.at[0]))
    for d in range(1, NX):
        S.send(x == 0, y0b, y0b, y0_sem.at[1], at(z, (x + d) % NX, c))

    mapped = mm_full(inv[...], x0[...].astype(F32))
    hi, lo = split(mapped)
    mh[0] = hi
    mh[1] = lo
    lst[...] = ls[...].T
    hi, lo = split(mm(ls[...], mh[0]) + mm(ls[...], mh[1]))
    wr[0] = hi
    wr[1] = lo

    def cols_block(b):
        keep = jnp.where((c == 0) & (b == 0), 0.0, 1.0).astype(F32)
        left = gt[b]
        v = mm(left, xr[...]) - keep * (mm(left, wr[0]) + mm(left, wr[1]))
        v = v.reshape(NZ, NX, 8, 256)
        for q in range(NX):
            part[q, b] = v[:, q].reshape(64, 256)

    def x_copy(src, dst, recv, which, i, device):
        return pltpu.make_async_remote_copy(
            src_ref=src, dst_ref=dst, send_sem=cs_sem.at[which, i], recv_sem=recv,
            device_id=device, device_id_type=MESH,
        )

    def step1(i):
        j = i + 4
        return (
            x_copy(pm1.at[i], rm1.at[i], m1_sem.at[i], 0, i, right),
            x_copy(pleft.at[i], rright.at[i], m2r_sem.at[i], 1, i, left_),
            x_copy(pm1.at[j], rm1.at[j], m1_sem.at[j], 2, i, left_),
            x_copy(pright.at[j], rleft.at[j], m2l_sem.at[j], 3, i, right),
        )

    def step2(i):
        j = i + 4
        return (
            x_copy(pright.at[i], rleft.at[i], m2l_sem.at[i], 4, i, right),
            x_copy(pleft.at[j], rright.at[j], m2r_sem.at[j], 5, i, left_),
        )

    def cols_step(i):
        cols_block(i)
        cols_block(i + 4)
        j = i + 4
        pm1[i] = part[xo_, i].astype(BF16)
        pleft[i] = part[xl_, i].astype(BF16)
        pm1[j] = part[xo_, j].astype(BF16)
        pright[j] = part[xr_, j].astype(BF16)
        for copy in step1(i):
            copy.start()

    def relay_upper(s):
        p = slot(s, xl_)
        arrived(p, ux_sem.at[0, s])
        S.send(s < 2, p, p, ux_sem.at[2, s], right)
        p = slot(s, xr_)
        arrived(p, ux_sem.at[1, s])
        S.send(s >= 2, p, p, ux_sem.at[2, s], left_)

    pl.loop(0, 4)(cols_step)
    relay_upper(far_s[0])
    relay_upper(far_s[1])
    relay_upper(far_s[2])
    relay_upper(far_s[3])

    for blk in range(2):
        rsl = pl.ds(blk * 256, 256)
        first_col = mm(gm[rsl, :256], xc[:256, :])
        rest = mm(gm[rsl, 256:], xc[256:, :])
        acc[rsl, :] = rest + first_col
        hi, lo = split(rest + keep_col * first_col)
        wc[0, rsl, :] = hi
        wc[1, rsl, :] = lo
    upper = mm(lst[...], wc[0, :512, :]) + mm(lst[...], wc[1, :512, :])
    invt = inv[...].T
    upper = -mm_full(invt, upper)
    for q in range(8):
        ub[q % 2, q // 2] = upper[q * 32:(q + 1) * 32, :]
    S.send(None, ub.at[1 - k], usib, up_sem.at[0], sib)

    def upper_y():
        arrived(usib, up_sem.at[0])
        uy[...] = ub[k] + usib[...]
        for d in range(1, NY):
            q = (y + d) % NY
            S.send(None, uy.at[q], uyr.at[y], upy_sem.at[y], at(z, x, 2 * q + k))

    def upper_z():
        v = uy[y]
        for d in range(1, NY):
            q = (y + d) % NY
            arrived(uyr.at[q], upy_sem.at[q])
            v = v + uyr[q]
        uz[...] = v
        S.send(z != 0, uz, uzr.at[z], upz_sem.at[z], at(0 * z, x, c))

    def upper_x():
        @pl.when(z == 0)
        def _():
            v = uz[...]
            for q in range(1, NZ):
                arrived(uzr.at[q], upz_sem.at[q])
                v = v + uzr[q]
            uf[...] = v

        S.send((z == 0) & (x != 0), uf, ufr.at[x], upf_sem.at[x], at(z, 0 * x, c))

    @pl.loop(0, 4)
    def _(i):
        j = i + 4
        arrived(rm1.at[i], m1_sem.at[i])
        pright[i] = (part[xr_, i] + rm1[i].astype(F32)).astype(BF16)
        arrived(rm1.at[j], m1_sem.at[j])
        pleft[j] = (part[xl_, j] + rm1[j].astype(F32)).astype(BF16)
        for copy in step2(i):
            copy.start()

    bcast_own(llo, 3, 0, 0)
    upper_y()

    for s in range(4):
        arrived(slot(s, xo_), ux_sem.at[2, s])
    low_sum = jnp.zeros((256, 256), F32)
    whole = ut[...].reshape(2048, 256)
    for blk in range(2):
        rsl = pl.ds(blk * 256, 256)
        keep = keep_row if blk == 0 else jnp.ones((), F32)
        hi, lo = split((mm(gm[rsl, :], whole) * keep).T)
        low_sum = low_sum + mm(hi, xr[rsl, :]) + mm(lo, xr[rsl, :])
    lower = -mm_full(invt, low_sum)
    lower = lower.reshape(NZ, NX, 8, 256)
    for q in range(NX):
        lx[q] = lower[:, q].reshape(64, 256).astype(BF16)
        lxf[q] = lower[:, q].reshape(64, 256)
    for d in range(1, NX):
        q = (x + d) % NX
        S.send(None, lx.at[q], lxr.at[x], lowx_sem.at[x], at(z, q, c))

    upper_z()

    def z_copy(i, d):
        zd = (z + d) % NZ
        return pltpu.make_async_remote_copy(
            src_ref=zs.at[zd, i], dst_ref=zr.at[z, i], send_sem=zss_sem.at[i, d], recv_sem=zr_sem.at[i, z],
            device_id=at(zd, x, c), device_id_type=MESH,
        )

    @pl.loop(0, 4)
    def _(i):
        for h in range(2):
            b = i + 4 * h
            arrived(rleft.at[b], m2l_sem.at[b])
            arrived(rright.at[b], m2r_sem.at[b])
            v = part[x, b] + rleft[b].astype(F32) + rright[b].astype(F32)
            v = v.reshape(NZ, 8, 256)
            zf[i, h] = v
            for q in range(NZ):
                zs[q, i, h] = v[q].astype(BF16)
        for d in range(1, NZ):
            z_copy(i, d).start()

    bcast_rest(llo, 3, 0, 0)

    @pl.loop(0, 8)
    def _(b):
        s = pl.ds(pl.multiple_of(b * 256, 256), 256)
        u = ut[b].reshape(256, 256)
        hi, lo = split(mm(u, mh[0]) + mm(u, mh[1]))
        wc[0, s, :] = hi
        wc[1, s, :] = lo

    for blk in range(2):
        rsl = pl.ds(blk * 256, 256)
        keep = keep_row if blk == 0 else jnp.ones((), F32)
        rows = acc[rsl, :] - keep * (mm(gm[rsl, :], wc[0]) + mm(gm[rsl, :], wc[1]))
        for q in range(8):
            rb[q % 2, q // 2, blk] = rows[q * 32:(q + 1) * 32, :]
    S.send(None, rb.at[1 - k], rsib, sib_sem.at[0], sib)

    for d in range(1, NX):
        arrived(lxr.at[(x + d) % NX], lowx_sem.at[(x + d) % NX])
    v = lxf[x] + lxr[xr_].astype(F32) + lxr[xo_].astype(F32) + lxr[xl_].astype(F32)
    lz[...] = v.reshape(NZ, 8, 256)
    for d in range(1, NZ):
        q = (z + d) % NZ
        S.send(None, lz.at[q], lzr.at[z], lowz_sem.at[z], at(q, x, c))

    upper_x()

    arrived(rsib, sib_sem.at[0])

    @pl.loop(0, 4)
    def _(q):
        v = rb[k, q] + rsib[q]
        rb[k, q] = v
        rys[q] = v.astype(BF16)

    for d in range(1, NY):
        q = (y + d) % NY
        S.send(None, rys.at[q], ryr.at[y], ry_sem.at[y], at(z, x, 2 * q + k))

    def update(b):
        u = ut[b].reshape(256, 256)
        dims = (((1,), (1,)), ((), ()))
        v = lax.dot_general(ls[...], u, dims, preferred_element_type=F32)
        v = v + lax.dot_general(llo[...], u, dims, preferred_element_type=F32)
        s = pl.ds(b, 512, stride=8)
        g32.at[0][s, :] = v[:, :128]
        g32.at[1][s, :] = v[:, 128:]

    bcast_end(llo, 3, 0, 0)
    update(0)
    update(1)

    v = lz[z]
    for d in range(1, NZ):
        q = (z + d) % NZ
        arrived(lzr.at[q], lowz_sem.at[q])
        v = v + lzr[q]
    lf[...] = v
    S.send(c != 0, lf, lfr.at[c], lowf_sem.at[c], at(z, x, 0 * c))
    update(2)
    update(3)
    pl.when(x != 0)(lambda: arrived(y0b, y0_sem.at[1]))
    solved = mm_full(y0b[...], inv[...].T)
    lower_full = ls[...].astype(F32) + llo[...].astype(F32)
    change = lax.dot_general(
        solved, lower_full, (((1,), (1,)), ((), ())), precision=HIGHEST, preferred_element_type=F32
    )
    red_out[0:1, :] = targets[0:1, :] - change[0:1, :256]
    red_out[1:2, :] = targets[1:2, :] - change[0:1, 256:]

    for b in range(4, 8):
        update(b)
    get_a.wait()
    put_a = [
        pltpu.make_async_copy(up.at[pl.ds(i * 1024, 1024)], up_out.at[pl.ds(i * 1024, 1024)], local_sem.at[4 + i])
        for i in range(4)
    ]
    for i in range(4):
        s = pl.ds(i * 1024, 1024)
        up[s, :128] = up[s, :128] - g32[0, s, :]
        up[s, 128:] = up[s, 128:] - g32[1, s, :]
        put_a[i].start()

    total = rb[k, y]
    for d in range(1, NY):
        q = (y + d) % NY
        arrived(ryr.at[q], ry_sem.at[q])
        total = total + ryr[q].astype(F32)
    rows_out[...] = total * scale

    for i in range(4):
        v = [zf[i, h, z] for h in range(2)]
        for d in range(1, NZ):
            q = (z + d) % NZ
            arrived(zr.at[q, i], zr_sem.at[i, q])
            for h in range(2):
                v[h] = v[h] + zr[q, i, h].astype(F32)
        cols_out[i] = v[0] * scale
        cols_out[i + 4] = v[1] * scale

    @pl.when(c == 0)
    def _():
        v = lf[...]
        for q in range(1, 8):
            arrived(lfr.at[q], lowf_sem.at[q])
            v = v + lfr[q]
        cols_out[0] = cols_out[0] + v * scale

    @pl.when((z == 0) & (x == 0))
    def _():
        v = uf[...]
        for q in range(1, NX):
            arrived(ufr.at[q], upf_sem.at[q])
            v = v + ufr[q]
        rows_out[0] = rows_out[0] + v * scale

    S.drain()

    @pl.loop(0, 4)
    def _(i):
        for copy in step1(i) + step2(i):
            copy.wait_send()
        for d in range(1, NZ):
            z_copy(i, d).wait_send()
    for copy in put_a:
        copy.wait()


def deliver(up, red, rows, cols, up_to, red_to, rows_to, cols_to, upv, redv, rowsv, colsv, sems):
    def part(ref, i):
        return ref.at[pl.ds(i * 512, 512)]

    pairs = [(part(up, i), part(upv, i), part(up_to, i)) for i in range(8)]
    pairs += [(red, redv, red_to), (rows, rowsv, rows_to), (cols, colsv, cols_to)]
    take = [pltpu.make_async_copy(src, mid, sems.at[0, i]) for i, (src, mid, _) in enumerate(pairs)]
    give = [pltpu.make_async_copy(mid, dst, sems.at[1, i]) for i, (_, mid, dst) in enumerate(pairs)]
    for copy in take:
        copy.start()
    for i in range(len(pairs)):
        take[i].wait()
        give[i].start()
    for copy in give:
        copy.wait()


def shards(trailing, inv_block, features, targets, cot_trailing):
    tr = trailing.reshape(4096, 256)
    g = cot_trailing.reshape(4096, 256)
    feats = features.reshape(2048, 256)
    vm = pl.BlockSpec(memory_space=pltpu.VMEM)
    hbm = pl.BlockSpec(memory_space=pltpu.HBM)
    V = pltpu.VMEM
    D = pltpu.SemaphoreType.DMA
    shapes = (
        jax.ShapeDtypeStruct((4096, 256), F32),
        jax.ShapeDtypeStruct((2, 256), F32),
        jax.ShapeDtypeStruct((2, 32, 256), F32),
        jax.ShapeDtypeStruct((8, 8, 256), F32),
    )
    results = pl.pallas_call(
        comm_kernel,
        out_shape=shapes,
        in_specs=[hbm, vm, hbm, vm, hbm],
        out_specs=(hbm, vm, vm, vm),
        scratch_shapes=[
            V((4096, 256), BF16), V((2, 4096, 128), F32), V((512, 2048), BF16), V((8, 256, 512), BF16),
            V((2048, 256), BF16), V((512, 256), BF16), V((512, 256), BF16), V((512, 256), BF16),
            V((256, 256), BF16), V((8, 2, 128, 256), BF16), V((8, 256), F32), V((4096, 256), F32),
            V((2, 512, 256), BF16), V((2, 2048, 256), BF16), V((2, 256, 256), BF16), V((256, 512), BF16),
            V((4, 8, 64, 256), F32), V((8, 64, 256), BF16), V((8, 64, 256), BF16), V((8, 64, 256), BF16),
            V((8, 64, 256), BF16), V((8, 64, 256), BF16), V((8, 64, 256), BF16),
            V((8, 4, 2, 8, 256), BF16), V((8, 4, 2, 8, 256), BF16), V((4, 2, 8, 8, 256), F32),
            V((2, 4, 2, 32, 256), F32), V((4, 2, 32, 256), F32), V((4, 2, 32, 256), BF16), V((4, 2, 32, 256), BF16),
            V((2, 4, 32, 256), F32), V((4, 32, 256), F32), V((4, 32, 256), F32), V((4, 32, 256), F32),
            V((32, 256), F32), V((8, 32, 256), F32), V((32, 256), F32), V((4, 32, 256), F32),
            V((4, 64, 256), BF16), V((4, 64, 256), BF16), V((4, 64, 256), F32), V((8, 8, 256), F32), V((8, 8, 256), F32),
            V((8, 256), F32), V((8, 8, 256), F32),
            V((512, 256), F32),
            D((9,)), D((140,)), D((4, 4)), D((1,)), D((4,)), D((3, 4)),
            D((6, 4)), D((8,)), D((8,)), D((8,)), D((4, 8)), D((4, 8)),
            D((1,)), D((4,)), D((1,)), D((4,)), D((8,)), D((4,)), D((4,)), D((8,)), D((8,)), D((2,)),
        ],
        compiler_params=pltpu.CompilerParams(
            collective_id=0, has_side_effects=True, vmem_limit_bytes=63 * 1024 * 1024
        ),
        name="panel_comm",
    )(tr, inv_block, feats, targets, g)
    updated, reduced, rows, cols = pl.pallas_call(
        deliver,
        out_shape=shapes,
        in_specs=[hbm] * 4,
        out_specs=(hbm,) * 4,
        scratch_shapes=[V(v.shape, v.dtype) for v in shapes] + [D((2, 11))],
        compiler_params=pltpu.CompilerParams(vmem_limit_bytes=63 * 1024 * 1024),
        name="deliver",
    )(*results)
    return (
        updated.reshape(trailing.shape),
        reduced,
        rows.reshape(2, 1, 32, 256),
        cols.reshape(8, 1, 8, 256),
    )


def solution(mesh):
    return jax.shard_map(
        shards,
        mesh=mesh,
        in_specs=(
            P(None, "row", None, "col"),
            P(),
            P(None, "col", None, None),
            P(None, "row"),
            P(None, "row", None, "col"),
        ),
        out_specs=(
            P(None, "row", None, "col"),
            P(None, "row"),
            P(None, "row", "col", None),
            P(None, "col", "row", None),
        ),
        check_vma=False,
    )
```

```python
import functools

import jax
import jax.numpy as jnp
from jax import lax
from jax.experimental import pallas as pl
from jax.experimental.pallas import tpu as pltpu
from jax.sharding import PartitionSpec as P

MESH = pl.DeviceIdType.MESH
F32 = jnp.float32
BF16 = jnp.bfloat16
HIGHEST = lax.Precision.HIGHEST
NX, NZ, NY = 4, 8, 4


def mm(a, b):
    return jnp.dot(a, b, preferred_element_type=F32)


def split(v):
    hi = v.astype(BF16)
    return hi, (v - hi.astype(F32)).astype(BF16)


def mm_full(a, b):
    ah, al = split(a)
    bh, bl = split(b)
    return mm(ah, bh) + (mm(ah, bl) + mm(al, bh))


class Sends:
    def __init__(self, sems):
        self.sems = sems
        self.used = 0
        self.copies = []

    def make(self, src, dst, recv, device, slot=None):
        if slot is None:
            slot = self.used
            self.used += 1
        return pltpu.make_async_remote_copy(
            src_ref=src, dst_ref=dst, send_sem=self.sems.at[slot], recv_sem=recv,
            device_id=device, device_id_type=MESH,
        )

    def send(self, pred, src, dst, recv, device):
        copy = self.make(src, dst, recv, device)
        self.copies.append((pred, copy))
        if pred is None:
            copy.start()
        else:
            pl.when(pred)(copy.start)

    def drain(self):
        for pred, copy in self.copies:
            if pred is None:
                copy.wait_send()
            else:
                pl.when(pred)(copy.wait_send)
        self.copies = []


def arrived(ref, sem):
    pltpu.make_async_copy(ref, ref, sem).wait()


def comm_kernel(
    tr, inv, feats, targets, g,
    up_out, red_out, rows_out, cols_out,
    g16, g32, gm, gt, xc, ls, llo, xr, x0, ut, y0b, up,
    wr, wc, mh, lst,
    part, pm1, pright, pleft, rm1, rleft, rright, zs, zr, zf,
    rb, rsib, rys, ryr,
    ub, usib, uy, uyr, uz, uzr, uf, ufr,
    lx, lxr, lxf, lz, lzr, lf, lfr,
    acc,
    local_sem, send_sem, s1_sem, ua_sem, uz_sem, ux_sem,
    cs_sem, m1_sem, m2l_sem, m2r_sem, zss_sem, zr_sem,
    sib_sem, ry_sem, up_sem, upy_sem, upz_sem, upf_sem, lowx_sem, lowz_sem, lowf_sem, y0_sem,
):
    r = lax.axis_index("row")
    c = lax.axis_index("col")
    z, x = r // NX, r % NX
    y, k = c // 2, c % 2
    xr_, xl_, xo_ = (x + 1) % NX, (x + 3) % NX, (x + 2) % NX

    def at(z_, x_, c_):
        return (z_ * NX + x_, c_)

    sib = at(z, x, 2 * y + 1 - k)
    S = Sends(send_sem)
    scale = 1.0 / feats.shape[1]

    get_g = pltpu.make_async_copy(g, g16, local_sem.at[0])
    get_f = pltpu.make_async_copy(feats, xc, local_sem.at[1])
    get_t = [pltpu.make_async_copy(tr.at[:, pl.ds(h * 128, 128)], g32.at[h], local_sem.at[2 + 6 * h]) for h in range(2)]

    @pl.when(c == 0)
    def _():
        get_t[0].start()
        get_t[1].start()

    get_f.start()
    get_a = pltpu.make_async_copy(tr, up, local_sem.at[3])

    @pl.when(c != 0)
    def _():
        get_g.start()
        get_a.start()

    def by_stride(b):
        s = pl.ds(b, 512, stride=8)
        return jnp.concatenate([g32.at[0][s, :], g32.at[1][s, :]], axis=1)

    bar = pltpu.get_barrier_semaphore()
    pl.semaphore_signal(bar, inc=1, device_id=sib, device_id_type=MESH)
    for d in range(1, NY):
        pl.semaphore_signal(bar, inc=1, device_id=at(z, x, 2 * ((y + d) % NY) + k), device_id_type=MESH)
    for d in range(1, NX):
        pl.semaphore_signal(bar, inc=1, device_id=at(z, (x + d) % NX, c), device_id_type=MESH)
    for d in range(1, NZ):
        pl.semaphore_signal(bar, inc=1, device_id=at((z + d) % NZ, x, c), device_id_type=MESH)
    srow = (z % 2) == (c // 4)
    home = c % 4
    cr = r % 8

    @pl.when(srow & jnp.logical_not((c == 0) & (x == home)))
    def _():
        pl.semaphore_signal(bar, inc=1, device_id=at(z, home, 0 * c), device_id_type=MESH)

    @pl.when(c == 0)
    def _():
        for q in (3, 5, 7):
            pl.semaphore_signal(bar, inc=1, device_id=at(z, x, q), device_id_type=MESH)

    @pl.when(c == 0)
    def _():
        get_t[0].wait()
        get_t[1].wait()
        low = mm_full(by_stride(0), inv[...].T)
        keep = jnp.where((r == 0) & (lax.broadcasted_iota(jnp.int32, (512, 256), 0) < 256), 0.0, 1.0)
        hi, lo = split(low * keep.astype(F32))
        ls[...] = hi
        llo[...] = lo

    pl.semaphore_wait(
        bar, 14 + jnp.where(c == 0, 4 - jnp.where(cr == 0, 1, 0), 0) + jnp.where((k == 1) & (c >= 3), 1, 0)
    )

    keep_row = jnp.where(r == 0, 0.0, 1.0).astype(F32)
    keep_col = jnp.where(c == 0, 0.0, 1.0).astype(F32)

    def piece(ref, q):
        n = ref.shape[0] // NY
        return ref.at[pl.ds(pl.multiple_of(q * n, n), n)]

    def bcast_root(ref, which, yr, kr):
        root = (y == yr) & (k == kr)
        sems = s1_sem.at[which]
        for d in range(1, NY):
            q = (yr + d) % NY
            S.send(root, piece(ref, q), piece(ref, q), sems.at[d], at(z, x, 2 * q + kr))
        for d in range(1, NY):
            q = (yr + d) % NY
            S.send(root, piece(ref, yr), piece(ref, yr), sems.at[0], at(z, x, 2 * q + kr))
        for d in range(NY):
            q = (yr + d) % NY
            S.send(root, piece(ref, q), piece(ref, q), sems.at[d], sib)

    def bcast_own(ref, which, yr, kr):
        relay = (y != yr) & (k == kr)
        sems = s1_sem.at[which]
        d0 = (y - yr + NY) % NY
        mine = piece(ref, y)
        pl.when(relay)(lambda: arrived(mine, sems.at[d0]))
        for e in (d0 % 3 + 1, (d0 + 1) % 3 + 1):
            S.send(relay, mine, mine, sems.at[d0], at(z, x, 2 * ((yr + e) % NY) + kr))
        S.send(relay, mine, mine, sems.at[d0], sib)

    def bcast_rest(ref, which, yr, kr):
        relay = (y != yr) & (k == kr)
        sems = s1_sem.at[which]
        d0 = (y - yr + NY) % NY
        for e in (d0 * 0, d0 % 3 + 1, (d0 + 1) % 3 + 1):
            p = piece(ref, (yr + e) % NY)
            pl.when(relay)(functools.partial(arrived, p, sems.at[e]))
            S.send(relay, p, p, sems.at[e], sib)

    def bcast_end(ref, which, yr, kr):
        @pl.when(k != kr)
        def _():
            for e in range(NY):
                arrived(piece(ref, (yr + e) % NY), s1_sem.at[which].at[e])

    yr2, kr2 = cr // 2, cr % 2
    b0 = r // 8
    mys = z // 2

    def slot(s, x_):
        return ut.at[s + 4 * (x_ // 2), x_ % 2]

    for q in range(NX):
        mine = (cr == 0) & (x == q)
        chunk = ls.at[pl.ds(q * 128, 128)]
        S.send((c == 0) & jnp.logical_not(mine), chunk, slot(mys, q), ua_sem.at[0], at(z, q, cr))

        @pl.when((c == 0) & mine)
        def _():
            ut[mys + 4 * (q // 2), q % 2] = chunk[...]

    bcast_root(ls, 0, 0, 0)
    get_f.wait()

    @pl.when(c == 0)
    def _():
        get_g.start()
        get_a.start()
        x0[...] = xc[pl.ds(0, 256), :]

    bcast_root(x0, 1, 0, 0)

    @pl.when(c == cr)
    def _():
        xr[pl.ds(0, 256), :] = xc[pl.ds(pl.multiple_of(b0 * 256, 256), 256), :]
        xr[pl.ds(256, 256), :] = xc[pl.ds(pl.multiple_of(b0 * 256 + 1024, 256), 256), :]

    bcast_root(xr, 2, yr2, kr2)

    first = (z == 0) & (x == 0)

    @pl.when(first)
    def _():
        y0b[...] = jnp.broadcast_to(targets[0:1, :], (8, 256))

    for d in range(1, NZ):
        S.send(first, y0b, y0b, y0_sem.at[0], at((z + d) % NZ, x, c))

    def relayout(b):
        v = by_stride(b).astype(BF16)
        gm[:, b * 256:(b + 1) * 256] = v
        gt[b] = v.T

    get_g.wait()

    @pl.loop(0, 8)
    def _(i):
        s = pl.ds(pl.multiple_of(i * 512, 512), 512)
        v = g16[s, :].astype(F32)
        g32[0, s, :] = v[:, :128]
        g32[1, s, :] = v[:, 128:]

    right, left_ = at(z, xr_, c), at(z, xl_, c)
    far_s = [((z + jnp.where(srow, near, off) + NZ) % NZ) // 2 for near, off in ((0, -1), (2, 1), (-2, 3), (4, -3))]

    def forward_upper(n):
        p = slot(far_s[n], x)
        if n == 0:
            pl.when(jnp.logical_not(srow))(lambda: arrived(p, uz_sem.at[far_s[0]]))
        else:
            arrived(p, uz_sem.at[far_s[n]])
        if n >= 2:
            step = 7 if n == 2 else 1
            hp = ut.at[far_s[n] + 4 * (x // 2), x % 2, pl.ds(64 * (n - 2), 64)]
            S.send(jnp.logical_not(srow), hp, hp, uz_sem.at[far_s[n]], at((z + step) % NZ, x, c))
        S.send(None, p, p, ux_sem.at[0, far_s[n]], right)
        S.send(None, p, p, ux_sem.at[1, far_s[n]], left_)

    own = slot(mys, x)
    pl.when(srow & jnp.logical_not((c == 0) & (x == home)))(lambda: arrived(own, ua_sem.at[0]))
    for d in (1, 7, 2, 6, 3, 5):
        S.send(srow, own, own, uz_sem.at[mys], at((z + d) % NZ, x, c))
    bcast_own(ls, 0, 0, 0)
    bcast_own(x0, 1, 0, 0)
    bcast_own(xr, 2, yr2, kr2)
    forward_upper(0)
    relayout(0)
    relayout(1)
    forward_upper(1)
    bcast_rest(ls, 0, 0, 0)
    bcast_rest(x0, 1, 0, 0)
    bcast_rest(xr, 2, yr2, kr2)
    relayout(2)
    relayout(3)
    forward_upper(2)
    relayout(4)
    relayout(5)
    forward_upper(3)
    relayout(6)
    relayout(7)
    bcast_end(ls, 0, 0, 0)
    bcast_end(x0, 1, 0, 0)
    bcast_end(xr, 2, yr2, kr2)

    bcast_root(llo, 3, 0, 0)

    pl.when((x == 0) & (z != 0))(lambda: arrived(y0b, y0_sem.at[0]))
    for d in range(1, NX):
        S.send(x == 0, y0b, y0b, y0_sem.at[1], at(z, (x + d) % NX, c))

    mapped = mm_full(inv[...], x0[...].astype(F32))
    hi, lo = split(mapped)
    mh[0] = hi
    mh[1] = lo
    w = mm(ls[...], mh[0]) + mm(ls[...], mh[1])
    hi, lo = split(xr[...].astype(F32) - w)
    wr[0, 0] = hi
    wr[0, 1] = lo
    hi, lo = split(xr[...].astype(F32) - keep_col * w)
    wr[1, 0] = hi
    wr[1, 1] = lo

    def cols_block(b):
        left = gt[b]
        which = jnp.where(b == 0, 1, 0)
        v = mm(left, wr[which, 0]) + mm(left, wr[which, 1])
        v = v.reshape(NZ, NX, 8, 256)
        for q in range(NX):
            part[q, b] = v[:, q].reshape(64, 256)

    def x_copy(src, dst, recv, which, i, device):
        return pltpu.make_async_remote_copy(
            src_ref=src, dst_ref=dst, send_sem=cs_sem.at[which, i], recv_sem=recv,
            device_id=device, device_id_type=MESH,
        )

    def step1(i):
        j = i + 4
        return (
            x_copy(pm1.at[i], rm1.at[i], m1_sem.at[i], 0, i, right),
            x_copy(pleft.at[i], rright.at[i], m2r_sem.at[i], 1, i, left_),
            x_copy(pm1.at[j], rm1.at[j], m1_sem.at[j], 2, i, left_),
            x_copy(pright.at[j], rleft.at[j], m2l_sem.at[j], 3, i, right),
        )

    def step2(i):
        j = i + 4
        return (
            x_copy(pright.at[i], rleft.at[i], m2l_sem.at[i], 4, i, right),
            x_copy(pleft.at[j], rright.at[j], m2r_sem.at[j], 5, i, left_),
        )

    def cols_step(i):
        cols_block(i)
        cols_block(i + 4)
        j = i + 4
        pm1[i] = part[xo_, i].astype(BF16)
        pleft[i] = part[xl_, i].astype(BF16)
        pm1[j] = part[xo_, j].astype(BF16)
        pright[j] = part[xr_, j].astype(BF16)
        for copy in step1(i):
            copy.start()

    def relay_upper(s):
        p = slot(s, xl_)
        arrived(p, ux_sem.at[0, s])
        S.send(s < 2, p, p, ux_sem.at[2, s], right)
        p = slot(s, xr_)
        arrived(p, ux_sem.at[1, s])
        S.send(s >= 2, p, p, ux_sem.at[2, s], left_)

    pl.loop(0, 4)(cols_step)
    relay_upper(far_s[0])
    relay_upper(far_s[1])
    relay_upper(far_s[2])
    relay_upper(far_s[3])

    for blk in range(2):
        rsl = pl.ds(blk * 256, 256)
        first_col = mm(gm[rsl, :256], xc[:256, :])
        rest = mm(gm[rsl, 256:], xc[256:, :])
        acc[rsl, :] = rest + first_col
        hi, lo = split(rest + keep_col * first_col)
        wc[0, rsl, :] = hi
        wc[1, rsl, :] = lo
    lst[...] = ls[...].T
    upper = mm(lst[...], wc[0, :512, :]) + mm(lst[...], wc[1, :512, :])
    invt = inv[...].T
    upper = -mm_full(invt, upper)
    for q in range(8):
        ub[q % 2, q // 2] = upper[q * 32:(q + 1) * 32, :]
    S.send(None, ub.at[1 - k], usib, up_sem.at[0], sib)

    def upper_y():
        arrived(usib, up_sem.at[0])
        uy[...] = ub[k] + usib[...]
        for d in range(1, NY):
            q = (y + d) % NY
            S.send(None, uy.at[q], uyr.at[y], upy_sem.at[y], at(z, x, 2 * q + k))

    def upper_z():
        v = uy[y]
        for d in range(1, NY):
            q = (y + d) % NY
            arrived(uyr.at[q], upy_sem.at[q])
            v = v + uyr[q]
        uz[...] = v
        S.send(z != 0, uz, uzr.at[z], upz_sem.at[z], at(0 * z, x, c))

    def upper_x():
        @pl.when(z == 0)
        def _():
            v = uz[...]
            for q in range(1, NZ):
                arrived(uzr.at[q], upz_sem.at[q])
                v = v + uzr[q]
            uf[...] = v

        S.send((z == 0) & (x != 0), uf, ufr.at[x], upf_sem.at[x], at(z, 0 * x, c))

    @pl.loop(0, 4)
    def _(i):
        j = i + 4
        arrived(rm1.at[i], m1_sem.at[i])
        pright[i] = (part[xr_, i] + rm1[i].astype(F32)).astype(BF16)
        arrived(rm1.at[j], m1_sem.at[j])
        pleft[j] = (part[xl_, j] + rm1[j].astype(F32)).astype(BF16)
        for copy in step2(i):
            copy.start()

    bcast_own(llo, 3, 0, 0)
    upper_y()

    S.drain()

    for s in range(4):
        arrived(slot(s, xo_), ux_sem.at[2, s])
    low_sum = jnp.zeros((256, 256), F32)
    whole = ut[...].reshape(2048, 256)
    for blk in range(2):
        rsl = pl.ds(blk * 256, 256)
        keep = keep_row if blk == 0 else jnp.ones((), F32)
        hi, lo = split((mm(gm[rsl, :], whole) * keep).T)
        low_sum = low_sum + mm(hi, xr[rsl, :]) + mm(lo, xr[rsl, :])
    lower = -mm_full(invt, low_sum)
    lower = lower.reshape(NZ, NX, 8, 256)
    for q in range(NX):
        lx[q] = lower[:, q].reshape(64, 256).astype(BF16)
        lxf[q] = lower[:, q].reshape(64, 256)
    for d in range(1, NX):
        q = (x + d) % NX
        S.send(None, lx.at[q], lxr.at[x], lowx_sem.at[x], at(z, q, c))

    upper_z()

    def z_copy(i, d):
        zd = (z + d) % NZ
        return pltpu.make_async_remote_copy(
            src_ref=zs.at[zd, i], dst_ref=zr.at[z, i], send_sem=zss_sem.at[i, d], recv_sem=zr_sem.at[i, z],
            device_id=at(zd, x, c), device_id_type=MESH,
        )

    @pl.loop(0, 4)
    def _(i):
        for h in range(2):
            b = i + 4 * h
            arrived(rleft.at[b], m2l_sem.at[b])
            arrived(rright.at[b], m2r_sem.at[b])
            v = part[x, b] + rleft[b].astype(F32) + rright[b].astype(F32)
            v = v.reshape(NZ, 8, 256)
            zf[i, h] = v
            for q in range(NZ):
                zs[q, i, h] = v[q].astype(BF16)
        for d in range(1, NZ):
            z_copy(i, d).start()

    bcast_rest(llo, 3, 0, 0)

    @pl.loop(0, 8)
    def _(b):
        s = pl.ds(pl.multiple_of(b * 256, 256), 256)
        u = ut[b].reshape(256, 256)
        hi, lo = split(mm(u, mh[0]) + mm(u, mh[1]))
        wc[0, s, :] = hi
        wc[1, s, :] = lo

    for blk in range(2):
        rsl = pl.ds(blk * 256, 256)
        keep = keep_row if blk == 0 else jnp.ones((), F32)
        rows = acc[rsl, :] - keep * (mm(gm[rsl, :], wc[0]) + mm(gm[rsl, :], wc[1]))
        for q in range(8):
            rb[q % 2, q // 2, blk] = rows[q * 32:(q + 1) * 32, :]
    S.send(None, rb.at[1 - k], rsib, sib_sem.at[0], sib)

    for d in range(1, NX):
        arrived(lxr.at[(x + d) % NX], lowx_sem.at[(x + d) % NX])
    v = lxf[x] + lxr[xr_].astype(F32) + lxr[xo_].astype(F32) + lxr[xl_].astype(F32)
    lz[...] = v.reshape(NZ, 8, 256)
    for d in range(1, NZ):
        q = (z + d) % NZ
        S.send(None, lz.at[q], lzr.at[z], lowz_sem.at[z], at(q, x, c))

    upper_x()

    arrived(rsib, sib_sem.at[0])

    @pl.loop(0, 4)
    def _(q):
        v = rb[k, q] + rsib[q]
        rb[k, q] = v
        rys[q] = v.astype(BF16)

    for d in range(1, NY):
        q = (y + d) % NY
        S.send(None, rys.at[q], ryr.at[y], ry_sem.at[y], at(z, x, 2 * q + k))

    def update(b):
        u = ut[b].reshape(256, 256)
        dims = (((1,), (1,)), ((), ()))
        v = lax.dot_general(ls[...], u, dims, preferred_element_type=F32)
        v = v + lax.dot_general(llo[...], u, dims, preferred_element_type=F32)
        s = pl.ds(b, 512, stride=8)
        g32.at[0][s, :] = v[:, :128]
        g32.at[1][s, :] = v[:, 128:]

    bcast_end(llo, 3, 0, 0)
    update(0)
    update(1)

    v = lz[z]
    for d in range(1, NZ):
        q = (z + d) % NZ
        arrived(lzr.at[q], lowz_sem.at[q])
        v = v + lzr[q]
    lf[...] = v
    S.send(c != 0, lf, lfr.at[c], lowf_sem.at[c], at(z, x, 0 * c))
    update(2)
    update(3)
    pl.when(x != 0)(lambda: arrived(y0b, y0_sem.at[1]))
    solved = mm_full(y0b[...], inv[...].T)
    lower_full = ls[...].astype(F32) + llo[...].astype(F32)
    change = lax.dot_general(
        solved, lower_full, (((1,), (1,)), ((), ())), precision=HIGHEST, preferred_element_type=F32
    )
    red_out[0:1, :] = targets[0:1, :] - change[0:1, :256]
    red_out[1:2, :] = targets[1:2, :] - change[0:1, 256:]

    for b in range(4, 8):
        update(b)
    get_a.wait()
    put_a = [
        pltpu.make_async_copy(up.at[pl.ds(i * 1024, 1024)], up_out.at[pl.ds(i * 1024, 1024)], local_sem.at[4 + i])
        for i in range(4)
    ]
    for i in range(4):
        s = pl.ds(i * 1024, 1024)
        up[s, :128] = up[s, :128] - g32[0, s, :]
        up[s, 128:] = up[s, 128:] - g32[1, s, :]
        put_a[i].start()

    S.drain()

    @pl.loop(0, 4)
    def _(i):
        for copy in step1(i) + step2(i):
            copy.wait_send()
        for d in range(1, NZ):
            z_copy(i, d).wait_send()

    total = rb[k, y]
    for d in range(1, NY):
        q = (y + d) % NY
        arrived(ryr.at[q], ry_sem.at[q])
        total = total + ryr[q].astype(F32)
    rows_out[...] = total * scale

    for i in range(4):
        v = [zf[i, h, z] for h in range(2)]
        for d in range(1, NZ):
            q = (z + d) % NZ
            arrived(zr.at[q, i], zr_sem.at[i, q])
            for h in range(2):
                v[h] = v[h] + zr[q, i, h].astype(F32)
        cols_out[i] = v[0] * scale
        cols_out[i + 4] = v[1] * scale

    @pl.when(c == 0)
    def _():
        v = lf[...]
        for q in range(1, 8):
            arrived(lfr.at[q], lowf_sem.at[q])
            v = v + lfr[q]
        cols_out[0] = cols_out[0] + v * scale

    @pl.when((z == 0) & (x == 0))
    def _():
        v = uf[...]
        for q in range(1, NX):
            arrived(ufr.at[q], upf_sem.at[q])
            v = v + ufr[q]
        rows_out[0] = rows_out[0] + v * scale

    S.drain()

    for copy in put_a:
        copy.wait()


def deliver(up, red, rows, cols, up_to, red_to, rows_to, cols_to, upv, redv, rowsv, colsv, sems):
    def part(ref, i):
        return ref.at[pl.ds(i * 1024, 1024)]

    pairs = [(part(up, i), part(upv, i), part(up_to, i)) for i in range(4)]
    pairs += [(red, redv, red_to), (rows, rowsv, rows_to), (cols, colsv, cols_to)]
    take = [pltpu.make_async_copy(src, mid, sems.at[0, i]) for i, (src, mid, _) in enumerate(pairs)]
    give = [pltpu.make_async_copy(mid, dst, sems.at[1, i]) for i, (_, mid, dst) in enumerate(pairs)]
    for copy in take[::-1]:
        copy.start()
    for i in reversed(range(len(pairs))):
        take[i].wait()
        give[i].start()
    for copy in give:
        copy.wait()


def shards(trailing, inv_block, features, targets, cot_trailing):
    tr = trailing.reshape(4096, 256)
    g = cot_trailing.reshape(4096, 256)
    feats = features.reshape(2048, 256)
    vm = pl.BlockSpec(memory_space=pltpu.VMEM)
    hbm = pl.BlockSpec(memory_space=pltpu.HBM)
    V = pltpu.VMEM
    D = pltpu.SemaphoreType.DMA
    shapes = (
        jax.ShapeDtypeStruct((4096, 256), F32),
        jax.ShapeDtypeStruct((2, 256), F32),
        jax.ShapeDtypeStruct((2, 32, 256), F32),
        jax.ShapeDtypeStruct((8, 8, 256), F32),
    )
    results = pl.pallas_call(
        comm_kernel,
        out_shape=shapes,
        in_specs=[hbm, vm, hbm, vm, hbm],
        out_specs=(hbm, vm, vm, vm),
        scratch_shapes=[
            V((4096, 256), BF16), V((2, 4096, 128), F32), V((512, 2048), BF16), V((8, 256, 512), BF16),
            V((2048, 256), BF16), V((512, 256), BF16), V((512, 256), BF16), V((512, 256), BF16),
            V((256, 256), BF16), V((8, 2, 128, 256), BF16), V((8, 256), F32), V((4096, 256), F32),
            V((2, 2, 512, 256), BF16), V((2, 2048, 256), BF16), V((2, 256, 256), BF16), V((256, 512), BF16),
            V((4, 8, 64, 256), F32), V((8, 64, 256), BF16), V((8, 64, 256), BF16), V((8, 64, 256), BF16),
            V((8, 64, 256), BF16), V((8, 64, 256), BF16), V((8, 64, 256), BF16),
            V((8, 4, 2, 8, 256), BF16), V((8, 4, 2, 8, 256), BF16), V((4, 2, 8, 8, 256), F32),
            V((2, 4, 2, 32, 256), F32), V((4, 2, 32, 256), F32), V((4, 2, 32, 256), BF16), V((4, 2, 32, 256), BF16),
            V((2, 4, 32, 256), F32), V((4, 32, 256), F32), V((4, 32, 256), F32), V((4, 32, 256), F32),
            V((32, 256), F32), V((8, 32, 256), F32), V((32, 256), F32), V((4, 32, 256), F32),
            V((4, 64, 256), BF16), V((4, 64, 256), BF16), V((4, 64, 256), F32), V((8, 8, 256), F32), V((8, 8, 256), F32),
            V((8, 256), F32), V((8, 8, 256), F32),
            V((512, 256), F32),
            D((9,)), D((140,)), D((4, 4)), D((1,)), D((4,)), D((3, 4)),
            D((6, 4)), D((8,)), D((8,)), D((8,)), D((4, 8)), D((4, 8)),
            D((1,)), D((4,)), D((1,)), D((4,)), D((8,)), D((4,)), D((4,)), D((8,)), D((8,)), D((2,)),
        ],
        compiler_params=pltpu.CompilerParams(
            collective_id=0, has_side_effects=True, vmem_limit_bytes=63 * 1024 * 1024
        ),
        name="panel_comm",
    )(tr, inv_block, feats, targets, g)
    updated, reduced, rows, cols = pl.pallas_call(
        deliver,
        out_shape=shapes,
        in_specs=[hbm] * 4,
        out_specs=(hbm,) * 4,
        scratch_shapes=[V(v.shape, v.dtype) for v in shapes] + [D((2, 7))],
        compiler_params=pltpu.CompilerParams(vmem_limit_bytes=63 * 1024 * 1024),
        name="deliver",
    )(*results)
    return (
        updated.reshape(trailing.shape),
        reduced,
        rows.reshape(2, 1, 32, 256),
        cols.reshape(8, 1, 8, 256),
    )


def solution(mesh):
    return jax.shard_map(
        shards,
        mesh=mesh,
        in_specs=(
            P(None, "row", None, "col"),
            P(),
            P(None, "col", None, None),
            P(None, "row"),
            P(None, "row", None, "col"),
        ),
        out_specs=(
            P(None, "row", None, "col"),
            P(None, "row"),
            P(None, "row", "col", None),
            P(None, "col", "row", None),
        ),
        check_vma=False,
    )
```

```python
import functools

import jax
import jax.numpy as jnp
from jax import lax
from jax.experimental import pallas as pl
from jax.experimental.pallas import tpu as pltpu
from jax.sharding import PartitionSpec as P

MESH = pl.DeviceIdType.MESH
F32 = jnp.float32
BF16 = jnp.bfloat16
HIGHEST = lax.Precision.HIGHEST
NX, NZ, NY = 4, 8, 4


def mm(a, b):
    return jnp.dot(a, b, preferred_element_type=F32)


def split(v):
    hi = v.astype(BF16)
    return hi, (v - hi.astype(F32)).astype(BF16)


def mm_full(a, b):
    ah, al = split(a)
    bh, bl = split(b)
    return mm(ah, bh) + (mm(ah, bl) + mm(al, bh))


class Sends:
    def __init__(self, sems):
        self.sems = sems
        self.used = 0
        self.copies = []

    def make(self, src, dst, recv, device, slot=None):
        if slot is None:
            slot = self.used
            self.used += 1
        return pltpu.make_async_remote_copy(
            src_ref=src, dst_ref=dst, send_sem=self.sems.at[slot], recv_sem=recv,
            device_id=device, device_id_type=MESH,
        )

    def send(self, pred, src, dst, recv, device):
        copy = self.make(src, dst, recv, device)
        self.copies.append((pred, copy))
        if pred is None:
            copy.start()
        else:
            pl.when(pred)(copy.start)

    def drain(self):
        for pred, copy in self.copies:
            if pred is None:
                copy.wait_send()
            else:
                pl.when(pred)(copy.wait_send)
        self.copies = []


def arrived(ref, sem):
    pltpu.make_async_copy(ref, ref, sem).wait()


def comm_kernel(
    tr, inv, feats, targets, g,
    up_out, red_out, rows_out, cols_out,
    g16, g32, gm, gt, xc, ls, llo, xr, x0, ut, y0b, up,
    wr, wc, mh, lst,
    part, pm1, pright, pleft, rm1, rleft, rright, zs, zr, zf,
    rb, rsib, rys, ryr,
    ub, usib, uy, uyr, uz, uzr, uf, ufr,
    lx, lxr, lxf, lz, lzr, lf, lfr,
    acc,
    local_sem, send_sem, s1_sem, ua_sem, uz_sem, ux_sem,
    cs_sem, m1_sem, m2l_sem, m2r_sem, zss_sem, zr_sem,
    sib_sem, ry_sem, up_sem, upy_sem, upz_sem, upf_sem, lowx_sem, lowz_sem, lowf_sem, y0_sem,
):
    r = lax.axis_index("row")
    c = lax.axis_index("col")
    z, x = r // NX, r % NX
    y, k = c // 2, c % 2
    xr_, xl_, xo_ = (x + 1) % NX, (x + 3) % NX, (x + 2) % NX

    def at(z_, x_, c_):
        return (z_ * NX + x_, c_)

    sib = at(z, x, 2 * y + 1 - k)
    S = Sends(send_sem)
    scale = 1.0 / feats.shape[1]

    get_g = pltpu.make_async_copy(g, g16, local_sem.at[0])
    get_f = pltpu.make_async_copy(feats, xc, local_sem.at[1])
    get_t = [pltpu.make_async_copy(tr.at[:, pl.ds(h * 128, 128)], g32.at[h], local_sem.at[2 + 6 * h]) for h in range(2)]

    @pl.when(c == 0)
    def _():
        get_t[0].start()
        get_t[1].start()

    get_f.start()
    get_a = pltpu.make_async_copy(tr, up, local_sem.at[3])

    @pl.when(c != 0)
    def _():
        get_g.start()
        get_a.start()

    def by_stride(b):
        s = pl.ds(b, 512, stride=8)
        return jnp.concatenate([g32.at[0][s, :], g32.at[1][s, :]], axis=1)

    bar = pltpu.get_barrier_semaphore()
    pl.semaphore_signal(bar, inc=1, device_id=sib, device_id_type=MESH)
    for d in range(1, NY):
        pl.semaphore_signal(bar, inc=1, device_id=at(z, x, 2 * ((y + d) % NY) + k), device_id_type=MESH)
    for d in range(1, NX):
        pl.semaphore_signal(bar, inc=1, device_id=at(z, (x + d) % NX, c), device_id_type=MESH)
    for d in range(1, NZ):
        pl.semaphore_signal(bar, inc=1, device_id=at((z + d) % NZ, x, c), device_id_type=MESH)
    srow = (z % 2) == (c // 4)
    home = c % 4
    cr = r % 8

    @pl.when(srow & jnp.logical_not((c == 0) & (x == home)))
    def _():
        pl.semaphore_signal(bar, inc=1, device_id=at(z, home, 0 * c), device_id_type=MESH)

    @pl.when(c == 0)
    def _():
        for q in (3, 5, 7):
            pl.semaphore_signal(bar, inc=1, device_id=at(z, x, q), device_id_type=MESH)

    @pl.when(c == 0)
    def _():
        get_t[0].wait()
        get_t[1].wait()
        low = mm_full(by_stride(0), inv[...].T)
        keep = jnp.where((r == 0) & (lax.broadcasted_iota(jnp.int32, (512, 256), 0) < 256), 0.0, 1.0)
        hi, lo = split(low * keep.astype(F32))
        ls[...] = hi
        llo[...] = lo

    pl.semaphore_wait(
        bar, 14 + jnp.where(c == 0, 4 - jnp.where(cr == 0, 1, 0), 0) + jnp.where((k == 1) & (c >= 3), 1, 0)
    )

    keep_row = jnp.where(r == 0, 0.0, 1.0).astype(F32)
    keep_col = jnp.where(c == 0, 0.0, 1.0).astype(F32)

    def piece(ref, q):
        n = ref.shape[0] // NY
        return ref.at[pl.ds(pl.multiple_of(q * n, n), n)]

    def bcast_root(ref, which, yr, kr):
        root = (y == yr) & (k == kr)
        sems = s1_sem.at[which]
        for d in range(1, NY):
            q = (yr + d) % NY
            S.send(root, piece(ref, q), piece(ref, q), sems.at[d], at(z, x, 2 * q + kr))
        for d in range(1, NY):
            q = (yr + d) % NY
            S.send(root, piece(ref, yr), piece(ref, yr), sems.at[0], at(z, x, 2 * q + kr))
        for d in range(NY):
            q = (yr + d) % NY
            S.send(root, piece(ref, q), piece(ref, q), sems.at[d], sib)

    def bcast_own(ref, which, yr, kr):
        relay = (y != yr) & (k == kr)
        sems = s1_sem.at[which]
        d0 = (y - yr + NY) % NY
        mine = piece(ref, y)
        pl.when(relay)(lambda: arrived(mine, sems.at[d0]))
        for e in (d0 % 3 + 1, (d0 + 1) % 3 + 1):
            S.send(relay, mine, mine, sems.at[d0], at(z, x, 2 * ((yr + e) % NY) + kr))
        S.send(relay, mine, mine, sems.at[d0], sib)

    def bcast_rest(ref, which, yr, kr):
        relay = (y != yr) & (k == kr)
        sems = s1_sem.at[which]
        d0 = (y - yr + NY) % NY
        for e in (d0 * 0, d0 % 3 + 1, (d0 + 1) % 3 + 1):
            p = piece(ref, (yr + e) % NY)
            pl.when(relay)(functools.partial(arrived, p, sems.at[e]))
            S.send(relay, p, p, sems.at[e], sib)

    def bcast_end(ref, which, yr, kr):
        @pl.when(k != kr)
        def _():
            for e in range(NY):
                arrived(piece(ref, (yr + e) % NY), s1_sem.at[which].at[e])

    yr2, kr2 = cr // 2, cr % 2
    b0 = r // 8
    mys = z // 2

    def slot(s, x_):
        return ut.at[s + 4 * (x_ // 2), x_ % 2]

    for q in range(NX):
        mine = (cr == 0) & (x == q)
        chunk = ls.at[pl.ds(q * 128, 128)]
        S.send((c == 0) & jnp.logical_not(mine), chunk, slot(mys, q), ua_sem.at[0], at(z, q, cr))

        @pl.when((c == 0) & mine)
        def _():
            ut[mys + 4 * (q // 2), q % 2] = chunk[...]

    bcast_root(ls, 0, 0, 0)
    get_f.wait()

    @pl.when(c == 0)
    def _():
        get_g.start()
        get_a.start()
        x0[...] = xc[pl.ds(0, 256), :]

    bcast_root(x0, 1, 0, 0)

    @pl.when(c == cr)
    def _():
        xr[pl.ds(0, 256), :] = xc[pl.ds(pl.multiple_of(b0 * 256, 256), 256), :]
        xr[pl.ds(256, 256), :] = xc[pl.ds(pl.multiple_of(b0 * 256 + 1024, 256), 256), :]

    bcast_root(xr, 2, yr2, kr2)

    first = (z == 0) & (x == 0)

    @pl.when(first)
    def _():
        y0b[...] = jnp.broadcast_to(targets[0:1, :], (8, 256))

    for d in range(1, NZ):
        S.send(first, y0b, y0b, y0_sem.at[0], at((z + d) % NZ, x, c))

    def relayout(b):
        v = by_stride(b).astype(BF16)
        gm[:, b * 256:(b + 1) * 256] = v
        gt[b] = v.T

    get_g.wait()

    @pl.loop(0, 8)
    def _(i):
        s = pl.ds(pl.multiple_of(i * 512, 512), 512)
        v = g16[s, :].astype(F32)
        g32[0, s, :] = v[:, :128]
        g32[1, s, :] = v[:, 128:]

    right, left_ = at(z, xr_, c), at(z, xl_, c)
    far_s = [((z + jnp.where(srow, near, off) + NZ) % NZ) // 2 for near, off in ((0, -1), (2, 1), (-2, 3), (4, -3))]

    def forward_upper(n):
        p = slot(far_s[n], x)
        if n == 0:
            pl.when(jnp.logical_not(srow))(lambda: arrived(p, uz_sem.at[far_s[0]]))
        else:
            arrived(p, uz_sem.at[far_s[n]])
        if n >= 2:
            step = 7 if n == 2 else 1
            hp = ut.at[far_s[n] + 4 * (x // 2), x % 2, pl.ds(64 * (n - 2), 64)]
            S.send(jnp.logical_not(srow), hp, hp, uz_sem.at[far_s[n]], at((z + step) % NZ, x, c))
        S.send(None, p, p, ux_sem.at[0, far_s[n]], right)
        S.send(None, p, p, ux_sem.at[1, far_s[n]], left_)

    own = slot(mys, x)
    pl.when(srow & jnp.logical_not((c == 0) & (x == home)))(lambda: arrived(own, ua_sem.at[0]))
    for d in (1, 7, 3, 5, 2, 6):
        S.send(srow, own, own, uz_sem.at[mys], at((z + d) % NZ, x, c))
    bcast_own(ls, 0, 0, 0)
    bcast_own(x0, 1, 0, 0)
    bcast_own(xr, 2, yr2, kr2)
    forward_upper(0)
    relayout(0)
    relayout(1)
    forward_upper(1)
    bcast_rest(ls, 0, 0, 0)
    bcast_rest(x0, 1, 0, 0)
    bcast_rest(xr, 2, yr2, kr2)
    relayout(2)
    relayout(3)
    forward_upper(2)
    relayout(4)
    relayout(5)
    forward_upper(3)
    relayout(6)
    relayout(7)
    bcast_end(ls, 0, 0, 0)
    bcast_end(x0, 1, 0, 0)
    bcast_end(xr, 2, yr2, kr2)

    bcast_root(llo, 3, 0, 0)

    pl.when((x == 0) & (z != 0))(lambda: arrived(y0b, y0_sem.at[0]))
    for d in range(1, NX):
        S.send(x == 0, y0b, y0b, y0_sem.at[1], at(z, (x + d) % NX, c))

    mapped = mm_full(inv[...], x0[...].astype(F32))
    hi, lo = split(mapped)
    mh[0] = hi
    mh[1] = lo
    w = mm(ls[...], mh[0]) + mm(ls[...], mh[1])
    hi, lo = split(xr[...].astype(F32) - w)
    wr[0, 0] = hi
    wr[0, 1] = lo
    hi, lo = split(xr[...].astype(F32) - keep_col * w)
    wr[1, 0] = hi
    wr[1, 1] = lo

    def cols_block(b):
        left = gt[b]
        which = jnp.where(b == 0, 1, 0)
        v = mm(left, wr[which, 0]) + mm(left, wr[which, 1])
        v = v.reshape(NZ, NX, 8, 256)
        for q in range(NX):
            part[q, b] = v[:, q].reshape(64, 256)

    def x_copy(src, dst, recv, which, i, device):
        return pltpu.make_async_remote_copy(
            src_ref=src, dst_ref=dst, send_sem=cs_sem.at[which, i], recv_sem=recv,
            device_id=device, device_id_type=MESH,
        )

    def step1(i):
        j = i + 4
        return (
            x_copy(pm1.at[i], rm1.at[i], m1_sem.at[i], 0, i, right),
            x_copy(pleft.at[i], rright.at[i], m2r_sem.at[i], 1, i, left_),
            x_copy(pm1.at[j], rm1.at[j], m1_sem.at[j], 2, i, left_),
            x_copy(pright.at[j], rleft.at[j], m2l_sem.at[j], 3, i, right),
        )

    def step2(i):
        j = i + 4
        return (
            x_copy(pright.at[i], rleft.at[i], m2l_sem.at[i], 4, i, right),
            x_copy(pleft.at[j], rright.at[j], m2r_sem.at[j], 5, i, left_),
        )

    def cols_step(i):
        cols_block(i)
        cols_block(i + 4)
        j = i + 4
        pm1[i] = part[xo_, i].astype(BF16)
        pleft[i] = part[xl_, i].astype(BF16)
        pm1[j] = part[xo_, j].astype(BF16)
        pright[j] = part[xr_, j].astype(BF16)
        for copy in step1(i):
            copy.start()

    def relay_upper(s):
        p = slot(s, xl_)
        arrived(p, ux_sem.at[0, s])
        S.send(s < 2, p, p, ux_sem.at[2, s], right)
        p = slot(s, xr_)
        arrived(p, ux_sem.at[1, s])
        S.send(s >= 2, p, p, ux_sem.at[2, s], left_)

    pl.loop(0, 4)(cols_step)
    relay_upper(far_s[0])
    relay_upper(far_s[1])
    relay_upper(far_s[2])
    relay_upper(far_s[3])

    for blk in range(2):
        rsl = pl.ds(blk * 256, 256)
        first_col = mm(gm[rsl, :256], xc[:256, :])
        rest = mm(gm[rsl, 256:], xc[256:, :])
        acc[rsl, :] = rest + first_col
        hi, lo = split(rest + keep_col * first_col)
        wc[0, rsl, :] = hi
        wc[1, rsl, :] = lo
    lst[...] = ls[...].T
    upper = mm(lst[...], wc[0, :512, :]) + mm(lst[...], wc[1, :512, :])
    invt = inv[...].T
    upper = -mm_full(invt, upper)
    for q in range(8):
        ub[q % 2, q // 2] = upper[q * 32:(q + 1) * 32, :]
    S.send(None, ub.at[1 - k], usib, up_sem.at[0], sib)

    def upper_y():
        arrived(usib, up_sem.at[0])
        uy[...] = ub[k] + usib[...]
        for d in range(1, NY):
            q = (y + d) % NY
            S.send(None, uy.at[q], uyr.at[y], upy_sem.at[y], at(z, x, 2 * q + k))

    def upper_z():
        v = uy[y]
        for d in range(1, NY):
            q = (y + d) % NY
            arrived(uyr.at[q], upy_sem.at[q])
            v = v + uyr[q]
        uz[...] = v
        S.send(z != 0, uz, uzr.at[z], upz_sem.at[z], at(0 * z, x, c))

    def upper_x():
        @pl.when(z == 0)
        def _():
            v = uz[...]
            for q in range(1, NZ):
                arrived(uzr.at[q], upz_sem.at[q])
                v = v + uzr[q]
            uf[...] = v

        S.send((z == 0) & (x != 0), uf, ufr.at[x], upf_sem.at[x], at(z, 0 * x, c))

    @pl.loop(0, 4)
    def _(i):
        j = i + 4
        arrived(rm1.at[i], m1_sem.at[i])
        pright[i] = (part[xr_, i] + rm1[i].astype(F32)).astype(BF16)
        arrived(rm1.at[j], m1_sem.at[j])
        pleft[j] = (part[xl_, j] + rm1[j].astype(F32)).astype(BF16)
        for copy in step2(i):
            copy.start()

    bcast_own(llo, 3, 0, 0)
    upper_y()

    S.drain()

    for s in range(4):
        arrived(slot(s, xo_), ux_sem.at[2, s])
    low_sum = jnp.zeros((256, 256), F32)
    whole = ut[...].reshape(2048, 256)
    for blk in range(2):
        rsl = pl.ds(blk * 256, 256)
        keep = keep_row if blk == 0 else jnp.ones((), F32)
        hi, lo = split((mm(gm[rsl, :], whole) * keep).T)
        low_sum = low_sum + mm(hi, xr[rsl, :]) + mm(lo, xr[rsl, :])
    lower = -mm_full(invt, low_sum)
    lower = lower.reshape(NZ, NX, 8, 256)
    for q in range(NX):
        lx[q] = lower[:, q].reshape(64, 256).astype(BF16)
        lxf[q] = lower[:, q].reshape(64, 256)
    for d in range(1, NX):
        q = (x + d) % NX
        S.send(None, lx.at[q], lxr.at[x], lowx_sem.at[x], at(z, q, c))

    upper_z()

    def z_copy(i, d):
        zd = (z + d) % NZ
        return pltpu.make_async_remote_copy(
            src_ref=zs.at[zd, i], dst_ref=zr.at[z, i], send_sem=zss_sem.at[i, d], recv_sem=zr_sem.at[i, z],
            device_id=at(zd, x, c), device_id_type=MESH,
        )

    @pl.loop(0, 4)
    def _(i):
        for h in range(2):
            b = i + 4 * h
            arrived(rleft.at[b], m2l_sem.at[b])
            arrived(rright.at[b], m2r_sem.at[b])
            v = part[x, b] + rleft[b].astype(F32) + rright[b].astype(F32)
            v = v.reshape(NZ, 8, 256)
            zf[i, h] = v
            for q in range(NZ):
                zs[q, i, h] = v[q].astype(BF16)
        for d in range(1, NZ):
            z_copy(i, d).start()

    bcast_rest(llo, 3, 0, 0)

    @pl.loop(0, 8)
    def _(b):
        s = pl.ds(pl.multiple_of(b * 256, 256), 256)
        u = ut[b].reshape(256, 256)
        hi, lo = split(mm(u, mh[0]) + mm(u, mh[1]))
        wc[0, s, :] = hi
        wc[1, s, :] = lo

    for blk in range(2):
        rsl = pl.ds(blk * 256, 256)
        keep = keep_row if blk == 0 else jnp.ones((), F32)
        rows = acc[rsl, :] - keep * (mm(gm[rsl, :], wc[0]) + mm(gm[rsl, :], wc[1]))
        for q in range(8):
            rb[q % 2, q // 2, blk] = rows[q * 32:(q + 1) * 32, :]
    S.send(None, rb.at[1 - k], rsib, sib_sem.at[0], sib)

    for d in range(1, NX):
        arrived(lxr.at[(x + d) % NX], lowx_sem.at[(x + d) % NX])
    v = lxf[x] + lxr[xr_].astype(F32) + lxr[xo_].astype(F32) + lxr[xl_].astype(F32)
    lz[...] = v.reshape(NZ, 8, 256)
    for d in range(1, NZ):
        q = (z + d) % NZ
        S.send(None, lz.at[q], lzr.at[z], lowz_sem.at[z], at(q, x, c))

    upper_x()

    arrived(rsib, sib_sem.at[0])

    @pl.loop(0, 4)
    def _(q):
        v = rb[k, q] + rsib[q]
        rb[k, q] = v
        rys[q] = v.astype(BF16)

    for d in range(1, NY):
        q = (y + d) % NY
        S.send(None, rys.at[q], ryr.at[y], ry_sem.at[y], at(z, x, 2 * q + k))

    def update(b):
        u = ut[b].reshape(256, 256)
        dims = (((1,), (1,)), ((), ()))
        v = lax.dot_general(ls[...], u, dims, preferred_element_type=F32)
        v = v + lax.dot_general(llo[...], u, dims, preferred_element_type=F32)
        s = pl.ds(b, 512, stride=8)
        g32.at[0][s, :] = v[:, :128]
        g32.at[1][s, :] = v[:, 128:]

    bcast_end(llo, 3, 0, 0)
    update(0)
    update(1)

    v = lz[z]
    for d in range(1, NZ):
        q = (z + d) % NZ
        arrived(lzr.at[q], lowz_sem.at[q])
        v = v + lzr[q]
    lf[...] = v
    S.send(c != 0, lf, lfr.at[c], lowf_sem.at[c], at(z, x, 0 * c))
    update(2)
    update(3)
    pl.when(x != 0)(lambda: arrived(y0b, y0_sem.at[1]))
    solved = mm_full(y0b[...], inv[...].T)
    lower_full = ls[...].astype(F32) + llo[...].astype(F32)
    change = lax.dot_general(
        solved, lower_full, (((1,), (1,)), ((), ())), precision=HIGHEST, preferred_element_type=F32
    )
    red_out[0:1, :] = targets[0:1, :] - change[0:1, :256]
    red_out[1:2, :] = targets[1:2, :] - change[0:1, 256:]

    for b in range(4, 8):
        update(b)
    get_a.wait()
    put_a = [
        pltpu.make_async_copy(up.at[pl.ds(i * 1024, 1024)], up_out.at[pl.ds(i * 1024, 1024)], local_sem.at[4 + i])
        for i in range(4)
    ]
    for i in range(4):
        s = pl.ds(i * 1024, 1024)
        up[s, :128] = up[s, :128] - g32[0, s, :]
        up[s, 128:] = up[s, 128:] - g32[1, s, :]
        put_a[i].start()

    S.drain()

    @pl.loop(0, 4)
    def _(i):
        for copy in step1(i) + step2(i):
            copy.wait_send()
        for d in range(1, NZ):
            z_copy(i, d).wait_send()

    total = rb[k, y]
    for d in range(1, NY):
        q = (y + d) % NY
        arrived(ryr.at[q], ry_sem.at[q])
        total = total + ryr[q].astype(F32)
    rows_out[...] = total * scale

    for i in range(4):
        v = [zf[i, h, z] for h in range(2)]
        for d in range(1, NZ):
            q = (z + d) % NZ
            arrived(zr.at[q, i], zr_sem.at[i, q])
            for h in range(2):
                v[h] = v[h] + zr[q, i, h].astype(F32)
        cols_out[i] = v[0] * scale
        cols_out[i + 4] = v[1] * scale

    @pl.when(c == 0)
    def _():
        v = lf[...]
        for q in range(1, 8):
            arrived(lfr.at[q], lowf_sem.at[q])
            v = v + lfr[q]
        cols_out[0] = cols_out[0] + v * scale

    @pl.when((z == 0) & (x == 0))
    def _():
        v = uf[...]
        for q in range(1, NX):
            arrived(ufr.at[q], upf_sem.at[q])
            v = v + ufr[q]
        rows_out[0] = rows_out[0] + v * scale

    S.drain()

    for copy in put_a:
        copy.wait()


def deliver(up, red, rows, cols, up_to, red_to, rows_to, cols_to, upv, redv, rowsv, colsv, sems):
    def part(ref, i):
        return ref.at[pl.ds(i * 1024, 1024)]

    pairs = [(part(up, i), part(upv, i), part(up_to, i)) for i in range(4)]
    pairs += [(red, redv, red_to), (rows, rowsv, rows_to), (cols, colsv, cols_to)]
    take = [pltpu.make_async_copy(src, mid, sems.at[0, i]) for i, (src, mid, _) in enumerate(pairs)]
    give = [pltpu.make_async_copy(mid, dst, sems.at[1, i]) for i, (_, mid, dst) in enumerate(pairs)]
    for copy in take[::-1]:
        copy.start()
    for i in reversed(range(len(pairs))):
        take[i].wait()
        give[i].start()
    for copy in give:
        copy.wait()


def shards(trailing, inv_block, features, targets, cot_trailing):
    tr = trailing.reshape(4096, 256)
    g = cot_trailing.reshape(4096, 256)
    feats = features.reshape(2048, 256)
    vm = pl.BlockSpec(memory_space=pltpu.VMEM)
    hbm = pl.BlockSpec(memory_space=pltpu.HBM)
    V = pltpu.VMEM
    D = pltpu.SemaphoreType.DMA
    shapes = (
        jax.ShapeDtypeStruct((4096, 256), F32),
        jax.ShapeDtypeStruct((2, 256), F32),
        jax.ShapeDtypeStruct((2, 32, 256), F32),
        jax.ShapeDtypeStruct((8, 8, 256), F32),
    )
    results = pl.pallas_call(
        comm_kernel,
        out_shape=shapes,
        in_specs=[hbm, vm, hbm, vm, hbm],
        out_specs=(hbm, vm, vm, vm),
        scratch_shapes=[
            V((4096, 256), BF16), V((2, 4096, 128), F32), V((512, 2048), BF16), V((8, 256, 512), BF16),
            V((2048, 256), BF16), V((512, 256), BF16), V((512, 256), BF16), V((512, 256), BF16),
            V((256, 256), BF16), V((8, 2, 128, 256), BF16), V((8, 256), F32), V((4096, 256), F32),
            V((2, 2, 512, 256), BF16), V((2, 2048, 256), BF16), V((2, 256, 256), BF16), V((256, 512), BF16),
            V((4, 8, 64, 256), F32), V((8, 64, 256), BF16), V((8, 64, 256), BF16), V((8, 64, 256), BF16),
            V((8, 64, 256), BF16), V((8, 64, 256), BF16), V((8, 64, 256), BF16),
            V((8, 4, 2, 8, 256), BF16), V((8, 4, 2, 8, 256), BF16), V((4, 2, 8, 8, 256), F32),
            V((2, 4, 2, 32, 256), F32), V((4, 2, 32, 256), F32), V((4, 2, 32, 256), BF16), V((4, 2, 32, 256), BF16),
            V((2, 4, 32, 256), F32), V((4, 32, 256), F32), V((4, 32, 256), F32), V((4, 32, 256), F32),
            V((32, 256), F32), V((8, 32, 256), F32), V((32, 256), F32), V((4, 32, 256), F32),
            V((4, 64, 256), BF16), V((4, 64, 256), BF16), V((4, 64, 256), F32), V((8, 8, 256), F32), V((8, 8, 256), F32),
            V((8, 256), F32), V((8, 8, 256), F32),
            V((512, 256), F32),
            D((9,)), D((140,)), D((4, 4)), D((1,)), D((4,)), D((3, 4)),
            D((6, 4)), D((8,)), D((8,)), D((8,)), D((4, 8)), D((4, 8)),
            D((1,)), D((4,)), D((1,)), D((4,)), D((8,)), D((4,)), D((4,)), D((8,)), D((8,)), D((2,)),
        ],
        compiler_params=pltpu.CompilerParams(
            collective_id=0, has_side_effects=True, vmem_limit_bytes=63 * 1024 * 1024
        ),
        name="panel_comm",
    )(tr, inv_block, feats, targets, g)
    updated, reduced, rows, cols = pl.pallas_call(
        deliver,
        out_shape=shapes,
        in_specs=[hbm] * 4,
        out_specs=(hbm,) * 4,
        scratch_shapes=[V(v.shape, v.dtype) for v in shapes] + [D((2, 7))],
        compiler_params=pltpu.CompilerParams(vmem_limit_bytes=63 * 1024 * 1024),
        name="deliver",
    )(*results)
    return (
        updated.reshape(trailing.shape),
        reduced,
        rows.reshape(2, 1, 32, 256),
        cols.reshape(8, 1, 8, 256),
    )


def solution(mesh):
    return jax.shard_map(
        shards,
        mesh=mesh,
        in_specs=(
            P(None, "row", None, "col"),
            P(),
            P(None, "col", None, None),
            P(None, "row"),
            P(None, "row", None, "col"),
        ),
        out_specs=(
            P(None, "row", None, "col"),
            P(None, "row"),
            P(None, "row", "col", None),
            P(None, "col", "row", None),
        ),
        check_vma=False,
    )
```
